128 devices in a mesh: gx: 16 (over z_lo, x, core), gy: 8 (over y, z_hi).
Axes of the slice: x: 4, y: 4, z: 4 (z_hi: 2, z_lo: 2; z = z_hi * 2 + z_lo), core: 2. Of those that a mesh axis runs over, the one named last changes fastest.
Arguments:
- features: bfloat16 [64, 128, 64, 128], P(None, 'gx', 'gy'), may hold values from -6 to 6
- cotangent: bfloat16 [64, 128, 64, 128], P(None, 'gx', 'gy'), may hold values from -6 to 6
- block_mask: int32 [16, 8, 16], P('gx', 'gy'), may hold values from 0 to 1, as said below
- kernel_one: bfloat16 [3, 3, 3, 64, 64], replicated, may hold values from -0.15625 to 0.15625
- kernel_two: bfloat16 [3, 3, 3, 64, 64], replicated, may hold values from -0.15625 to 0.15625
Outputs:
- grad_features: bfloat16 [64, 128, 64, 128], P(None, 'gx', 'gy')
- grad_one: float32 [3, 3, 3, 64, 64], replicated
- grad_two: float32 [3, 3, 3, 64, 64], replicated
The draws below stay inside these ranges and needn't reach their ends.
Inputs may be any that keep to these rules, and one draw needn't show every extreme that they name: `block_mask`: 1 marks an active block of 8 x 8 x 8 cells, 0 an empty one.
All inputs are finite; a program needn't handle non-finite values.
Results may differ from the reference program's by a relative error of at most 0.0032.
Values may be sent and summed in bfloat16 or wider, within the bound.
No kernel may reach another device: no remote copies, remote signals or barrier semaphores. Data moves between devices by JAX's collectives and lax.ppermute only.
A program may use at most 192 MiB of HBM per device.

```python
import math
import jax
import jax.numpy as jnp
from jax import lax

C = 64
BS = 8
NX = 128
NY = 64
NZ = 128


def draw_block_mask(key, part):
    shape = (NX // BS, NY // BS, NZ // BS)
    rolls = jax.random.randint(key, shape, 0, 64)
    column = lax.broadcasted_iota(jnp.int32, shape, 0)
    limit = 24 + 36 * column // max(NX // BS - 1, 1)
    return (rolls < limit).astype(jnp.int32)


def block_levels(key, dims, split, smallest, top_value):
    gain, own = 1.0, jax.random.fold_in(key, 6)
    for axis_at, blocks in split:
        heights = jnp.exp(jax.random.uniform(jax.random.fold_in(own, axis_at), (blocks,), jnp.float32, smallest / len(split), top_value / len(split)))
        gain = gain * jnp.repeat(heights, dims[axis_at] // blocks).reshape([-1 if axis == axis_at else 1 for axis in range(len(dims))])
    return gain


def bell_draw(rng, shape, spread, bound, cuts=(), kind=jnp.bfloat16):
    drawn = spread * jax.random.normal(rng, shape, jnp.float32)
    if cuts:
        drawn = drawn * block_levels(rng, shape, cuts, -0.22, 0.18)
    return jnp.clip(drawn, -bound, bound).astype(kind)


def setup_inputs(seed: int = 0) -> dict:
    arg_keys = jax.random.split(jax.random.key(seed), 6)
    features = bell_draw(arg_keys[0], (C, NX, NY, NZ), 1.0, 6.0, ((1, 16), (2, 8)))
    cotangent = bell_draw(arg_keys[1], (C, NX, NY, NZ), 1.0, 6.0, ((1, 16), (2, 8)))
    block_mask = draw_block_mask(jax.random.fold_in(arg_keys[5], 71), 0)
    kernel_one = bell_draw(arg_keys[3], (3, 3, 3, C, C), (27 * C) ** -0.5, 0.15625)
    kernel_two = bell_draw(arg_keys[4], (3, 3, 3, C, C), (27 * C) ** -0.5, 0.15625)
    return dict(features=features, cotangent=cotangent, block_mask=block_mask, kernel_one=kernel_one, kernel_two=kernel_two)


def upsample(block_mask):
    nbx, nby, nbz = block_mask.shape
    wide = jnp.broadcast_to(block_mask[:, None, :, None, :, None], (nbx, BS, nby, BS, nbz, BS))
    return wide.reshape(nbx * BS, nby * BS, nbz * BS)

def flip_kernel(kernel):
    return jnp.transpose(jnp.flip(kernel, (0, 1, 2)), (0, 1, 2, 4, 3))

def silu_slope(value):
    sig = jax.nn.sigmoid(value)
    return sig * (1.0 + value * (1.0 - sig))

def plane_window(padded, index, width_y, width_z):
    slab = lax.dynamic_slice_in_dim(padded, index, 3, 1)
    parts = []
    for row_off in range(3):
        for col_off in range(3):
            for dep_off in range(3):
                parts.append(slab[:, row_off, col_off:col_off + width_y, dep_off:dep_off + width_z])
    return jnp.concatenate(parts, 0)

def conv_full(source, kernel):
    width_x, width_y, width_z = source.shape[1:]
    padded = jnp.pad(source.astype(jnp.float32), ((0, 0), (1, 1), (1, 1), (1, 1)))
    weights = kernel.astype(jnp.float32).reshape(27 * kernel.shape[3], kernel.shape[4])

    def plane(index):
        window = plane_window(padded, index, width_y, width_z)
        return jnp.einsum('jo,jyz->oyz', weights, window)
    planes = lax.map(plane, jnp.arange(width_x, dtype=jnp.int32))
    return jnp.transpose(planes, (1, 0, 2, 3))

def kernel_grad(source, grad):
    width_x, width_y, width_z = source.shape[1:]
    padded = jnp.pad(source.astype(jnp.float32), ((0, 0), (1, 1), (1, 1), (1, 1)))

    def plane(index):
        window = plane_window(padded, index, width_y, width_z)
        grad_plane = lax.dynamic_slice_in_dim(grad, index, 1, 1)[:, 0].astype(jnp.float32)
        return jnp.einsum('jyz,oyz->jo', window, grad_plane)
    terms = lax.map(plane, jnp.arange(width_x, dtype=jnp.int32))
    total = lax.optimization_barrier(jnp.sum(terms, 0))
    return total.reshape(3, 3, 3, source.shape[0], grad.shape[0])

def reference(features, cotangent, block_mask, kernel_one, kernel_two):
    cell = upsample(block_mask).astype(jnp.bfloat16)[None]
    cell_f = cell.astype(jnp.float32)
    masked_in = features * cell
    masked_grad = cotangent * cell
    pre_act = conv_full(masked_in, kernel_one)
    activ = (cell_f * jax.nn.silu(pre_act)).astype(jnp.bfloat16)
    act_grad = conv_full(masked_grad, flip_kernel(kernel_two))
    pre_grad = (cell_f * silu_slope(pre_act) * act_grad).astype(jnp.bfloat16)
    scale = 1.0 / math.sqrt(NX * NY * NZ)
    grad_two = kernel_grad(activ, masked_grad) * scale
    grad_one = kernel_grad(masked_in, pre_grad) * scale
    branch = conv_full(pre_grad, flip_kernel(kernel_one))
    grad_features = (cell_f * (cotangent.astype(jnp.float32) + branch)).astype(jnp.bfloat16)
    return (grad_features, grad_one, grad_two)
```

```python
import math

import jax
import jax.numpy as jnp
from jax import lax
from jax.experimental import pallas as pl
from jax.experimental.pallas import tpu as pltpu
from jax.sharding import PartitionSpec as P

F32 = jnp.float32
BF16 = jnp.bfloat16
AXES = ("gx", "gy")
PAIRS = 4


def shift_perm(count, step):
    return [(i, i + step) for i in range(count) if 0 <= i + step < count]


def xor_permute(value, mask):
    total = lax.axis_size("gx") * lax.axis_size("gy")
    return lax.ppermute(value, AXES, [(i, i ^ mask) for i in range(total)])


def stack_row(stack, at_x, first_y, row):
    count, chans, depth = row.shape
    lane = lax.broadcasted_iota(jnp.int32, row.shape, 2)
    zero = jnp.zeros_like(row)
    below = jnp.where(lane == 0, zero, pltpu.roll(row, 1, 2))
    above = jnp.where(lane == depth - 1, zero, pltpu.roll(row, depth - 1, 2))
    ys = pl.ds(first_y, count)
    stack[at_x, ys, 0:chans, :] = below
    stack[at_x, ys, chans : 2 * chans, :] = row
    stack[at_x, ys, 2 * chans : 3 * chans, :] = above


def stack_padded(stack, tile, x_lo, x_hi, y_lo, y_hi, c_lo, c_hi):
    size_x, size_y = tile.shape[0], tile.shape[1]
    stack_row(stack, 0, 1, x_lo[...])
    stack_row(stack, size_x + 1, 1, x_hi[...])
    for edge in range(2):
        at_x = edge * (size_x + 1)
        stack_row(stack, at_x, 0, c_lo[pl.ds(edge, 1)])
        stack_row(stack, at_x, size_y + 1, c_hi[pl.ds(edge, 1)])

    def body(i, carry):
        stack_row(stack, i + 1, 1, tile[i])
        stack_row(stack, i + 1, 0, y_lo[pl.ds(i, 1)])
        stack_row(stack, i + 1, size_y + 1, y_hi[pl.ds(i, 1)])
        return carry

    lax.fori_loop(0, size_x, body, 0)


def conv_stack(stack, weights, acc):
    wide, tall, deep, depth = stack.shape
    chans = deep // 3
    acc[0:2] = jnp.zeros((2,) + acc.shape[1:], F32)

    def body(i, carry):
        for pair in range((tall - 2) // 2):
            y = 2 * pair
            left = stack[i, y : y + 3].reshape(3 * deep, depth)
            right = stack[i, y + 1 : y + 4].reshape(3 * deep, depth)
            both = jnp.concatenate([left, right], axis=1)
            out = jnp.dot(weights[...], both, preferred_element_type=F32)
            for side in range(2):
                part = out[:, side * depth : (side + 1) * depth]
                acc[i + 2, y + side] = part[0:chans]
                acc[i + 1, y + side] += part[chans : 2 * chans]
                acc[i, y + side] += part[2 * chans : 3 * chans]
        return carry

    lax.fori_loop(0, wide, body, 0)


def forward_kernel(mask, weights, tile, x_lo, x_hi, y_lo, y_hi, c_lo, c_hi, activ, slope, padded, stack, acc):
    stack_padded(stack, tile, x_lo, x_hi, y_lo, y_hi, c_lo, c_hi)
    chans = tile.shape[2]
    padded[...] = stack[:, :, chans : 2 * chans, :]
    conv_stack(stack, weights, acc)

    def body(i, carry):
        value = acc[i + 2]
        sig = jax.nn.sigmoid(value)
        activ[i] = (mask[...] * (value * sig)).astype(BF16)
        slope[i] = mask[...] * (sig * (1.0 + value * (1.0 - sig)))
        return carry

    lax.fori_loop(0, tile.shape[0], body, 0)


def backward_kernel(
    weights, slope, tile, x_lo, x_hi, y_lo, y_hi, c_lo, c_hi, pre_grad, p_ylo, p_yhi, padded, stack, acc
):
    stack_padded(stack, tile, x_lo, x_hi, y_lo, y_hi, c_lo, c_hi)
    size_x, size_y, chans = tile.shape[0:3]
    padded[...] = stack[:, :, chans : 2 * chans, :]
    conv_stack(stack, weights, acc)

    def body(i, carry):
        value = (slope[i] * acc[i + 2]).astype(BF16)
        pre_grad[i] = value
        p_ylo[i] = value[0]
        p_yhi[i] = value[size_y - 1]
        return carry

    lax.fori_loop(0, size_x, body, 0)


def branch_kernel(mask, weights, base, tile, x_lo, x_hi, y_lo, y_hi, c_lo, c_hi, result, stack, acc):
    stack_padded(stack, tile, x_lo, x_hi, y_lo, y_hi, c_lo, c_hi)
    conv_stack(stack, weights, acc)

    def body(i, carry):
        result[i] = (base[i].astype(F32) + mask[...] * acc[i + 2]).astype(BF16)
        return carry

    lax.fori_loop(0, tile.shape[0], body, 0)


def grad_accumulate(padded, stack, acc, turned):
    size_x, size_y, deep, depth = stack.shape
    chans = deep // 3
    acc[...] = jnp.zeros_like(acc)

    def body(i, carry):
        right = jnp.concatenate([stack[i, y] for y in range(size_y)], axis=1)
        left = []
        for a in range(3):
            rows = [padded[i + a, y] for y in range(size_y + 2)]
            for b in range(3):
                left.append(jnp.concatenate(rows[b : b + size_y], axis=1))
        left = jnp.concatenate(left, axis=0)
        acc[...] += lax.dot_general(left, right, (((1,), (1,)), ((), ())), preferred_element_type=F32)
        return carry

    lax.fori_loop(0, size_x, body, 0)


def pack_grad(dest, acc, chans):
    rows = acc.shape[0]
    half = rows // 2
    dest[0:rows] = acc[:, 0 : 2 * chans]
    low = acc[0:half, 2 * chans : 3 * chans]
    high = acc[half:rows, 2 * chans : 3 * chans]
    dest[rows : rows + half] = jnp.concatenate([low, high], axis=1)


def grads_kernel(core, in_pad, pre_grad, grad_pad, activ, keep, send, stack, acc_one, acc_two):
    size_x, size_y, chans = activ.shape[0:3]

    def stack_all(source):
        def body(i, carry):
            stack_row(stack, i, 0, source[i])
            return carry

        lax.fori_loop(0, size_x, body, 0)

    stack_all(activ)
    grad_accumulate(grad_pad, stack, acc_two, True)
    stack_all(pre_grad)
    grad_accumulate(in_pad, stack, acc_one, False)

    @pl.when(core[0] == 0)
    def _():
        pack_grad(keep, acc_one, chans)
        pack_grad(send, acc_two, chans)

    @pl.when(core[0] != 0)
    def _():
        pack_grad(keep, acc_two, chans)
        pack_grad(send, acc_one, chans)


def split_kernel(spot, keep, recv, *outs):
    rows = outs[0].shape[0]
    for dist, out in enumerate(outs):
        start = pl.multiple_of((spot[0] ^ dist) * rows, 8)
        out[...] = keep[pl.ds(start, rows)] + recv[pl.ds(start, rows)]


def join_kernel(spot, *refs):
    out = refs[-1]
    rows = refs[0].shape[0]
    for dist, part in enumerate(refs[:-1]):
        start = pl.multiple_of((spot[0] ^ dist) * rows, 8)
        out[pl.ds(start, rows)] = part[...]


def unpack_kernel(core, scale, own, other, grad_one, grad_two):
    chans = grad_one.shape[-1]
    rows = 9 * chans
    half = rows // 2

    def block(source, a, b, j):
        start = (3 * a + b) * chans
        if j < 2:
            return source[start : start + chans, j * chans : (j + 1) * chans]
        pieces = []
        step = chans // 2
        for first in (start, start + step):
            if first < half:
                pieces.append(source[rows + first : rows + first + step, 0:chans])
            else:
                pieces.append(source[rows + first - half : rows + first - half + step, chans : 2 * chans])
        return jnp.concatenate(pieces, axis=0)

    def write(one, two):
        for a in range(3):
            for b in range(3):
                for j in range(3):
                    grad_one[a, b, 2 - j] = block(one, a, b, j) * scale
                    grad_two[2 - a, 2 - b, j] = block(two, a, b, j).T * scale

    @pl.when(core[0] == 0)
    def _():
        write(own, other)

    @pl.when(core[0] != 0)
    def _():
        write(other, own)


def call(kernel, outs, scratch=(), scalars=0, flops=0, name=None):
    def run(*operands):
        specs = [pl.BlockSpec(memory_space=pltpu.SMEM)] * scalars
        specs += [pl.BlockSpec(memory_space=pltpu.VMEM)] * (len(operands) - scalars)
        moved = sum(o.size * o.dtype.itemsize for o in operands)
        moved += sum(math.prod(o.shape) * o.dtype.itemsize for o in outs)
        return pl.pallas_call(
            kernel,
            out_shape=tuple(outs),
            in_specs=specs,
            out_specs=tuple(pl.BlockSpec(memory_space=pltpu.VMEM) for _ in outs),
            scratch_shapes=list(scratch),
            cost_estimate=pl.CostEstimate(flops=flops, bytes_accessed=moved, transcendentals=0),
            compiler_params=pltpu.CompilerParams(vmem_limit_bytes=40 * 1024 * 1024),
            name=name,
        )(*operands)

    return run


def halo(x_lo, x_hi, y_lo, y_hi):
    nx, ny = lax.axis_size("gx"), lax.axis_size("gy")
    got_ylo = lax.ppermute(y_hi, "gy", shift_perm(ny, 1))
    got_yhi = lax.ppermute(y_lo, "gy", shift_perm(ny, -1))
    got_xlo = lax.ppermute(x_hi, "gx", shift_perm(nx, 1))
    got_xhi = lax.ppermute(x_lo, "gx", shift_perm(nx, -1))
    first = jnp.stack([got_xlo[0], got_xhi[0]])
    last = jnp.stack([got_xlo[-1], got_xhi[-1]])
    got_clo = lax.ppermute(last, "gy", shift_perm(ny, 1))
    got_chi = lax.ppermute(first, "gy", shift_perm(ny, -1))
    return got_xlo, got_xhi, got_ylo, got_yhi, got_clo, got_chi


def shards(features, cotangent, block_mask, kernel_one, kernel_two):
    chans, tile_x, tile_y, tile_z = features.shape
    blocks = block_mask.shape[2]
    cells_all = tile_x * tile_y * tile_z * lax.axis_size("gx") * lax.axis_size("gy")
    scale = 1.0 / math.sqrt(cells_all)
    place_x, place_y = lax.axis_index("gx"), lax.axis_index("gy")
    core = (place_x & 1).astype(jnp.int32).reshape(1)
    spot = ((place_x >> 1) & 3).astype(jnp.int32).reshape(1)

    mask = jnp.broadcast_to(block_mask.reshape(blocks, 1), (blocks, tile_z // blocks)).reshape(1, tile_z)
    mask_f = mask.astype(F32)
    mask_b = mask.astype(BF16).reshape(1, 1, 1, tile_z)
    masked_in = jnp.transpose(features * mask_b, (1, 2, 0, 3))
    masked_grad = jnp.transpose(cotangent * mask_b, (1, 2, 0, 3))

    def edges(tile):
        return tile[0], tile[-1], tile[:, 0], tile[:, -1]

    in_halo = halo(*edges(masked_in))
    grad_halo = halo(*edges(masked_grad))

    w_pre = jnp.transpose(kernel_one, (0, 4, 1, 2, 3)).reshape(3 * chans, 9 * chans)
    flat = lambda w: jnp.transpose(w[::-1, ::-1, ::-1], (0, 3, 1, 2, 4)).reshape(3 * chans, 9 * chans)
    w_act = flat(kernel_two)
    w_branch = flat(kernel_one)

    tile_shape = (tile_x, tile_y, chans, tile_z)
    pad_shape = (tile_x + 2, tile_y + 2, chans, tile_z)
    scratch = [
        pltpu.VMEM((tile_x + 2, tile_y + 2, 3 * chans, tile_z), BF16),
        pltpu.VMEM((tile_x + 4, tile_y, chans, tile_z), F32),
    ]
    tile_b = jax.ShapeDtypeStruct(tile_shape, BF16)
    edge_b = jax.ShapeDtypeStruct((tile_x, chans, tile_z), BF16)
    pad_b = jax.ShapeDtypeStruct(pad_shape, BF16)
    flops = 2 * 27 * chans * chans * tile_x * tile_y * tile_z

    activ, slope, in_pad = call(
        forward_kernel,
        [tile_b, jax.ShapeDtypeStruct(tile_shape, F32), pad_b],
        scratch,
        flops=flops,
        name="pre_act",
    )(mask_f, w_pre, masked_in, *in_halo)
    pre_grad, p_ylo, p_yhi, grad_pad = call(
        backward_kernel, [tile_b, edge_b, edge_b, pad_b], scratch, flops=flops, name="act_grad"
    )(w_act, slope, masked_grad, *grad_halo)
    pre_halo = halo(pre_grad[0], pre_grad[-1], p_ylo, p_yhi)

    packed = 27 * chans * chans // (2 * chans)
    half = jax.ShapeDtypeStruct((packed, 2 * chans), F32)
    keep, send = call(
        grads_kernel,
        [half, half],
        [
            pltpu.VMEM((tile_x, tile_y, 3 * chans, tile_z), BF16),
            pltpu.VMEM((9 * chans, 3 * chans), F32),
            pltpu.VMEM((9 * chans, 3 * chans), F32),
        ],
        scalars=1,
        flops=2 * flops,
        name="grads",
    )(core, in_pad, pre_grad, grad_pad, activ)

    recv = xor_permute(send, 8)
    chunk = jax.ShapeDtypeStruct((packed // 4, 2 * chans), F32)
    parts = call(split_kernel, [chunk] * 4, scalars=1, name="split")(spot, keep, recv)
    parts = [parts[0]] + [xor_permute(parts[d], 16 * d) for d in range(1, 4)]
    part = (parts[0] + parts[1]) + (parts[2] + parts[3])
    for masks in ((2, 4, 6), (1, 64, 65)):
        near, mid, far = [xor_permute(part, m) for m in masks]
        part = (part + near) + (mid + far)
    pieces = [part] + [xor_permute(part, 16 * d) for d in range(1, 4)]
    (own,) = call(join_kernel, [half], scalars=1, name="join")(spot, *pieces)
    other = xor_permute(own, 8)
    grad_shape = jax.ShapeDtypeStruct((3, 3, 3, chans, chans), F32)

    def unpack(core_ref, own_ref, other_ref, one_ref, two_ref):
        unpack_kernel(core_ref, scale, own_ref, other_ref, one_ref, two_ref)

    grad_one, grad_two = call(unpack, [grad_shape, grad_shape], scalars=1, name="unpack")(core, own, other)

    (branch,) = call(branch_kernel, [tile_b], scratch, flops=flops, name="branch")(
        mask_f, w_branch, masked_grad, pre_grad, *pre_halo
    )
    grad_features = jnp.transpose(branch, (2, 0, 1, 3))
    return grad_features, grad_one, grad_two


def solution(mesh):
    placed = (P(None, "gx", "gy", None), P(None, "gx", "gy", None), P("gx", "gy", None), P(), P())
    return jax.shard_map(
        shards,
        mesh=mesh,
        in_specs=placed,
        out_specs=(P(None, "gx", "gy", None), P(), P()),
        check_vma=False,
    )
```

```python
import functools
import math

import jax
import jax.numpy as jnp
from jax import lax
from jax.experimental import pallas as pl
from jax.experimental.pallas import tpu as pltpu
from jax.sharding import PartitionSpec as P


F32 = jnp.float32
BF16 = jnp.bfloat16
AXES = ("gx", "gy")


def swap_perms(count):
    even = [(i, i ^ 1) for i in range(count)]
    odd = [(i, i + 1 if i % 2 else i - 1) for i in range(1, count - 1)]
    return even, odd


def xor_permute(value, mask):
    total = lax.axis_size("gx") * lax.axis_size("gy")
    return lax.ppermute(value, AXES, [(i, i ^ mask) for i in range(total)])


def swap(value_even, value_odd, axis):
    even, odd = swap_perms(lax.axis_size(axis))
    return lax.ppermute(value_even, axis, even), lax.ppermute(value_odd, axis, odd)


def stack_row(stack, at_x, first_y, row):
    count, chans, depth = row.shape
    lane = lax.broadcasted_iota(jnp.int32, row.shape, 2)
    zero = jnp.zeros_like(row)
    below = jnp.where(lane == 0, zero, pltpu.roll(row, 1, 2))
    above = jnp.where(lane == depth - 1, zero, pltpu.roll(row, depth - 1, 2))
    ys = pl.ds(first_y, count)
    stack[at_x, ys, 0:chans, :] = below
    stack[at_x, ys, chans : 2 * chans, :] = row
    stack[at_x, ys, 2 * chans : 3 * chans, :] = above


def sides(parity, size):
    even = (1 - parity) * (size + 1)
    return even, size + 1 - even


def stack_padded(stack, place, tile, xr_even, xr_odd, yr_even, yr_odd, which):
    size_x, size_y = tile.shape[0], tile.shape[1]
    x_even, x_odd = sides(place[0], size_x)
    y_even, y_odd = sides(place[1], size_y)
    stack_row(stack, x_even, 1, xr_even[which])
    stack_row(stack, x_odd, 1, xr_odd[which])

    def column(i, carry):
        stack_row(stack, i, y_even, yr_even[pl.ds(i, 1)])
        stack_row(stack, i, y_odd, yr_odd[pl.ds(i, 1)])
        return carry

    lax.fori_loop(0, size_x + 2, column, 0)

    def body(i, carry):
        stack_row(stack, i + 1, 1, tile[i])
        return carry

    lax.fori_loop(0, size_x, body, 0)


def ypack_kernel(place, tile, xr_even, xr_odd, ys_even, ys_odd, *, which):
    size_x, size_y = tile.shape[0], tile.shape[1]
    x_even, x_odd = sides(place[0], size_x)
    for out, edge in ((ys_even, (1 - place[1]) * (size_y - 1)), (ys_odd, place[1] * (size_y - 1))):
        out[x_even] = xr_even[which, edge]
        out[x_odd] = xr_odd[which, edge]
        for i in range(size_x):
            out[i + 1] = tile[i, edge]


def conv_stack(stack, weights, acc, first=0):
    wide, _, deep, depth = stack.shape
    tall = acc.shape[1]
    chans = deep // 3
    acc[0:2] = jnp.zeros((2,) + acc.shape[1:], F32)

    def body(i, carry):
        for y in range(0, tall, 2):
            at = first + y
            left = stack[i, at : at + 3].reshape(3 * deep, depth)
            right = stack[i, at + 1 : at + 4].reshape(3 * deep, depth)
            both = jnp.concatenate([left, right], axis=1)
            out = jnp.dot(weights[...], both, preferred_element_type=F32)
            for side in range(2):
                part = out[:, side * depth : (side + 1) * depth]
                acc[i + 2, y + side] = part[0:chans]
                acc[i + 1, y + side] += part[chans : 2 * chans]
                acc[i, y + side] += part[2 * chans : 3 * chans]
        return carry

    lax.fori_loop(0, wide, body, 0)


def forward_kernel(place, mask, weights, tile, xr_even, xr_odd, yr_even, yr_odd, activ, slope, padded, stack, acc):
    stack_padded(stack, place, tile, xr_even, xr_odd, yr_even, yr_odd, 0)
    chans = tile.shape[2]
    padded[...] = stack[:, :, chans : 2 * chans, :]
    conv_stack(stack, weights, acc)

    def body(i, carry):
        value = acc[i + 2]
        sig = jax.nn.sigmoid(value)
        activ[i] = (mask[...] * (value * sig)).astype(BF16)
        slope[i] = mask[...] * (sig * (1.0 + value * (1.0 - sig)))
        return carry

    lax.fori_loop(0, tile.shape[0], body, 0)


def backward_kernel(
    place, weights, slope, tile, xr_even, xr_odd, yr_even, yr_odd, pre_grad, xs_even, xs_odd, padded, stack, acc
):
    stack_padded(stack, place, tile, xr_even, xr_odd, yr_even, yr_odd, 1)
    size_x, _, chans = tile.shape[0:3]
    padded[...] = stack[:, :, chans : 2 * chans, :]
    conv_stack(stack, weights, acc)

    def body(i, carry):
        pre_grad[i] = (slope[i] * acc[i + 2]).astype(BF16)
        return carry

    lax.fori_loop(0, size_x, body, 0)
    xs_even[0] = pre_grad[(1 - place[0]) * (size_x - 1)]
    xs_odd[0] = pre_grad[place[0] * (size_x - 1)]


def branch_finish(mask, base, result, acc, first):
    tall = acc.shape[1]

    def body(i, carry):
        result[i] = (base[i, first : first + tall].astype(F32) + mask[...] * acc[i + 2]).astype(BF16)
        return carry

    lax.fori_loop(0, base.shape[0], body, 0)


def branch_low_kernel(place, mask, weights, base, tile, xr_even, xr_odd, yr_even, yr_odd, result, stack, acc):
    stack_padded(stack, place, tile, xr_even, xr_odd, yr_even, yr_odd, 0)
    conv_stack(stack, weights, acc, 0)
    branch_finish(mask, base, result, acc, 0)


def branch_high_kernel(mask, weights, base, stack, result, acc):
    first = base.shape[1] // 2
    conv_stack(stack, weights, acc, first)
    branch_finish(mask, base, result, acc, first)


def grad_accumulate(padded, stack, acc):
    size_x, size_y, _, _ = stack.shape
    acc[...] = jnp.zeros_like(acc)

    def body(i, carry):
        right = jnp.concatenate([stack[i, y] for y in range(size_y)], axis=1)
        left = []
        for a in range(3):
            rows = [padded[i + a, y] for y in range(size_y + 2)]
            for b in range(3):
                left.append(jnp.concatenate(rows[b : b + size_y], axis=1))
        left = jnp.concatenate(left, axis=0)
        acc[...] += lax.dot_general(left, right, (((1,), (1,)), ((), ())), preferred_element_type=F32)
        return carry

    lax.fori_loop(0, size_x, body, 0)


def pack_grad(dest, acc, chans):
    rows = acc.shape[0]
    half = rows // 2
    dest[0:rows] = acc[:, 0 : 2 * chans]
    low = acc[0:half, 2 * chans : 3 * chans]
    high = acc[half:rows, 2 * chans : 3 * chans]
    dest[rows : rows + half] = jnp.concatenate([low, high], axis=1)


def stack_tile(stack, source):
    def body(i, carry):
        stack_row(stack, i, 0, source[i])
        return carry

    lax.fori_loop(0, source.shape[0], body, 0)


def grad_two_kernel(grad_pad, activ, packed, stack, acc):
    stack_tile(stack, activ)
    grad_accumulate(grad_pad, stack, acc)
    pack_grad(packed, acc, activ.shape[2])


def grad_one_kernel(place, in_pad, pre_grad, packed_two, keep, send, stack, acc):
    stack_tile(stack, pre_grad)
    grad_accumulate(in_pad, stack, acc)

    @pl.when(place[0] == 0)
    def _():
        pack_grad(keep, acc, pre_grad.shape[2])
        send[...] = packed_two[...]

    @pl.when(place[0] != 0)
    def _():
        pack_grad(send, acc, pre_grad.shape[2])
        keep[...] = packed_two[...]


def split_kernel(place, keep, recv, *outs):
    rows = outs[0].shape[0]
    for dist, out in enumerate(outs):
        start = pl.multiple_of((place[2] ^ dist) * rows, 8)
        out[...] = keep[pl.ds(start, rows)] + recv[pl.ds(start, rows)]


def join_kernel(place, *refs):
    out = refs[-1]
    rows = refs[0].shape[0]
    for dist, part in enumerate(refs[:-1]):
        start = pl.multiple_of((place[2] ^ dist) * rows, 8)
        out[pl.ds(start, rows)] = part[...]


def unpack_kernel(place, scale, own, other, grad_one, grad_two):
    chans = grad_one.shape[-1]
    rows = 9 * chans
    half = rows // 2

    def block(source, a, b, j):
        start = (3 * a + b) * chans
        if j < 2:
            return source[start : start + chans, j * chans : (j + 1) * chans]
        pieces = []
        step = chans // 2
        for first in (start, start + step):
            if first < half:
                pieces.append(source[rows + first : rows + first + step, 0:chans])
            else:
                pieces.append(source[rows + first - half : rows + first - half + step, chans : 2 * chans])
        return jnp.concatenate(pieces, axis=0)

    def write(one, two):
        for a in range(3):
            for b in range(3):
                for j in range(3):
                    grad_one[a, b, 2 - j] = block(one, a, b, j) * scale
                    grad_two[2 - a, 2 - b, j] = block(two, a, b, j).T * scale

    @pl.when(place[0] == 0)
    def _():
        write(own, other)

    @pl.when(place[0] != 0)
    def _():
        write(other, own)


def call(kernel, outs, scratch=(), scalars=0, flops=0):
    def run(*operands):
        specs = [pl.BlockSpec(memory_space=pltpu.SMEM)] * scalars
        specs += [pl.BlockSpec(memory_space=pltpu.VMEM)] * (len(operands) - scalars)
        moved = sum(o.size * o.dtype.itemsize for o in operands)
        moved += sum(math.prod(o.shape) * o.dtype.itemsize for o in outs)
        return pl.pallas_call(
            kernel,
            out_shape=tuple(outs),
            in_specs=specs,
            out_specs=tuple(pl.BlockSpec(memory_space=pltpu.VMEM) for _ in outs),
            scratch_shapes=list(scratch),
            cost_estimate=pl.CostEstimate(flops=flops, bytes_accessed=moved, transcendentals=0),
            compiler_params=pltpu.CompilerParams(vmem_limit_bytes=40 * 1024 * 1024),
        )(*operands)

    return run


def body(features, cotangent, block_mask, kernel_one, kernel_two):
    chans, tile_x, tile_y, tile_z = features.shape
    blocks = block_mask.shape[2]
    cells_all = tile_x * tile_y * tile_z * lax.axis_size("gx") * lax.axis_size("gy")
    scale = 1.0 / math.sqrt(cells_all)
    place_x, place_y = lax.axis_index("gx"), lax.axis_index("gy")
    x_odd, y_odd = place_x & 1, place_y & 1
    place = jnp.stack([x_odd, y_odd, (place_x >> 1) & 3]).astype(jnp.int32)

    mask = jnp.broadcast_to(block_mask.reshape(blocks, 1), (blocks, tile_z // blocks)).reshape(1, tile_z)
    mask_f = mask.astype(F32)
    mask_b = mask.astype(BF16).reshape(1, 1, tile_z)

    def x_edges(at):
        both = [lax.dynamic_index_in_dim(a, at, 1, keepdims=False) * mask_b for a in (features, cotangent)]
        return jnp.stack([jnp.transpose(a, (1, 0, 2)) for a in both])

    xr = swap(x_edges((1 - x_odd) * (tile_x - 1)), x_edges(x_odd * (tile_x - 1)), "gx")
    masked_in = jnp.transpose(features * mask_b[:, None], (1, 2, 0, 3))
    masked_grad = jnp.transpose(cotangent * mask_b[:, None], (1, 2, 0, 3))

    tile_shape = (tile_x, tile_y, chans, tile_z)
    tile_b = jax.ShapeDtypeStruct(tile_shape, BF16)
    column_b = jax.ShapeDtypeStruct((tile_x + 2, chans, tile_z), BF16)
    edge_b = jax.ShapeDtypeStruct((1, tile_y, chans, tile_z), BF16)
    pad_b = jax.ShapeDtypeStruct((tile_x + 2, tile_y + 2, chans, tile_z), BF16)
    flops = 2 * 27 * chans * chans * tile_x * tile_y * tile_z

    def y_sends(tile, halo_x, which):
        kernel = functools.partial(ypack_kernel, which=which)
        return call(kernel, [column_b] * 2, scalars=1)(place, tile, *halo_x)

    in_sends = y_sends(masked_in, xr, 0)
    grad_sends = y_sends(masked_grad, xr, 1)
    in_y = swap(*in_sends, "gy")
    grad_y = swap(*grad_sends, "gy")

    w_pre = jnp.transpose(kernel_one, (0, 4, 1, 2, 3)).reshape(3 * chans, 9 * chans)
    flat = lambda w: jnp.transpose(w[::-1, ::-1, ::-1], (0, 3, 1, 2, 4)).reshape(3 * chans, 9 * chans)
    w_pre, w_act, w_branch = lax.optimization_barrier((w_pre, flat(kernel_two), flat(kernel_one)))

    stack_s = pltpu.VMEM((tile_x + 2, tile_y + 2, 3 * chans, tile_z), BF16)
    stack_o = jax.ShapeDtypeStruct((tile_x + 2, tile_y + 2, 3 * chans, tile_z), BF16)
    acc_s = pltpu.VMEM((tile_x + 4, tile_y, chans, tile_z), F32)
    acc_h = pltpu.VMEM((tile_x + 4, tile_y // 2, chans, tile_z), F32)
    tile_s = pltpu.VMEM((tile_x, tile_y, 3 * chans, tile_z), BF16)
    grad_s = pltpu.VMEM((9 * chans, 3 * chans), F32)

    activ, slope, in_pad = call(
        forward_kernel, [tile_b, jax.ShapeDtypeStruct(tile_shape, F32), pad_b], [stack_s, acc_s], scalars=1, flops=flops
    )(place, mask_f, w_pre, masked_in, *xr, *in_y)
    pre_grad, xs_even, xs_odd, grad_pad = call(
        backward_kernel, [tile_b, edge_b, edge_b, pad_b], [stack_s, acc_s], scalars=1, flops=flops
    )(place, w_act, slope, masked_grad, *xr, *grad_y)

    packed = 27 * chans * chans // (2 * chans)
    half = jax.ShapeDtypeStruct((packed, 2 * chans), F32)
    pre_xr = swap(xs_even, xs_odd, "gx")
    (packed_two,) = call(grad_two_kernel, [half], [tile_s, grad_s], flops=flops)(grad_pad, activ)
    pre_sends = y_sends(pre_grad, pre_xr, 0)
    pre_yr = swap(*pre_sends, "gy")
    keep, send = call(grad_one_kernel, [half, half], [tile_s, grad_s], scalars=1, flops=flops)(
        place, in_pad, pre_grad, packed_two
    )

    recv = xor_permute(send, 8)
    chunk = jax.ShapeDtypeStruct((packed // 4, 2 * chans), F32)
    parts = call(split_kernel, [chunk] * 4, scalars=1)(place, keep, recv)
    parts = [parts[0]] + [xor_permute(parts[d], 16 * d) for d in range(1, 4)]
    part = (parts[0] + parts[1]) + (parts[2] + parts[3])
    for masks in ((2, 4, 6), (1, 64, 65)):
        near, mid, far = [xor_permute(part, m) for m in masks]
        part = (part + near) + (mid + far)
    pieces = [part] + [xor_permute(part, 16 * d) for d in range(1, 4)]
    (own,) = call(join_kernel, [half], scalars=1)(place, *pieces)
    other = xor_permute(own, 8)
    grad_shape = jax.ShapeDtypeStruct((3, 3, 3, chans, chans), F32)

    def unpack(place_ref, own_ref, other_ref, one_ref, two_ref):
        unpack_kernel(place_ref, scale, own_ref, other_ref, one_ref, two_ref)

    grad_one, grad_two = call(unpack, [grad_shape, grad_shape], scalars=1)(place, own, other)

    half_b = jax.ShapeDtypeStruct((tile_x, tile_y // 2, chans, tile_z), BF16)
    low, stacked = call(
        branch_low_kernel, [half_b, stack_o], [acc_h], scalars=1, flops=flops // 2
    )(place, mask_f, w_branch, masked_grad, pre_grad, *pre_xr, *pre_yr)
    (high,) = call(branch_high_kernel, [half_b], [acc_h], flops=flops // 2)(mask_f, w_branch, masked_grad, stacked)
    grad_features = jnp.transpose(jnp.concatenate([low, high], axis=1), (2, 0, 1, 3))
    return grad_features, grad_one, grad_two


def solution(mesh):
    placed = (P(None, "gx", "gy", None), P(None, "gx", "gy", None), P("gx", "gy", None), P(), P())
    return jax.shard_map(
        body,
        mesh=mesh,
        in_specs=placed,
        out_specs=(P(None, "gx", "gy", None), P(), P()),
        check_vma=False,
    )
```

```python
import functools
import math

import jax
import jax.numpy as jnp
from jax import lax
from jax.experimental import pallas as pl
from jax.experimental.pallas import tpu as pltpu
from jax.sharding import PartitionSpec as P


F32 = jnp.float32
BF16 = jnp.bfloat16
AXES = ("gx", "gy")


def swap_perms(count):
    even = [(i, i ^ 1) for i in range(count)]
    odd = [(i, i + 1 if i % 2 else i - 1) for i in range(1, count - 1)]
    return even, odd


def xor_permute(value, mask):
    total = lax.axis_size("gx") * lax.axis_size("gy")
    return lax.ppermute(value, AXES, [(i, i ^ mask) for i in range(total)])


def swap(value_even, value_odd, axis):
    even, odd = swap_perms(lax.axis_size(axis))
    return lax.ppermute(value_even, axis, even), lax.ppermute(value_odd, axis, odd)


def stack_row(stack, at_x, first_y, row):
    count, chans, depth = row.shape
    lane = lax.broadcasted_iota(jnp.int32, row.shape, 2)
    zero = jnp.zeros_like(row)
    below = jnp.where(lane == 0, zero, pltpu.roll(row, 1, 2))
    above = jnp.where(lane == depth - 1, zero, pltpu.roll(row, depth - 1, 2))
    ys = pl.ds(first_y, count)
    stack[at_x, ys, 0:chans, :] = below
    stack[at_x, ys, chans : 2 * chans, :] = row
    stack[at_x, ys, 2 * chans : 3 * chans, :] = above


def sides(parity, size):
    even = (1 - parity) * (size + 1)
    return even, size + 1 - even


def pad_tile(padded, place, tile, xr_even, xr_odd, yr_even, yr_odd, which):
    size_x, size_y = tile.shape[0], tile.shape[1]
    x_even, x_odd = sides(place[0], size_x)
    y_even, y_odd = sides(place[1], size_y)
    padded[x_even, 1 : size_y + 1] = xr_even[which]
    padded[x_odd, 1 : size_y + 1] = xr_odd[which]
    for i in range(size_x + 2):
        padded[i, y_even] = yr_even[i]
        padded[i, y_odd] = yr_odd[i]

    def body(i, carry):
        padded[i + 1, 1 : size_y + 1] = tile[i]
        return carry

    lax.fori_loop(0, size_x, body, 0)


def ypack_kernel(place, tile, xr_even, xr_odd, ys_even, ys_odd, *, which):
    size_x, size_y = tile.shape[0], tile.shape[1]
    x_even, x_odd = sides(place[0], size_x)
    for out, edge in ((ys_even, (1 - place[1]) * (size_y - 1)), (ys_odd, place[1] * (size_y - 1))):
        out[x_even] = xr_even[which, edge]
        out[x_odd] = xr_odd[which, edge]
        for i in range(size_x):
            out[i + 1] = tile[i, edge]


def conv_padded(padded, weights, first, count, emit):
    wide, _, chans, depth = padded.shape

    def body(x, carry):
        lane = lax.broadcasted_iota(jnp.int32, (chans, depth), 1)
        for y in range(first, first + count, 2):
            halves = []
            for side in range(2):
                at = y + side
                rows = [padded[x + a, at : at + 3].reshape(3 * chans, depth) for a in range(3)]
                halves.append(jnp.concatenate(rows, axis=0))
            out = jnp.dot(weights[...], jnp.concatenate(halves, axis=1), preferred_element_type=F32)
            for side in range(2):
                part = out[:, side * depth : (side + 1) * depth]
                below = jnp.where(lane == 0, 0.0, pltpu.roll(part[0:chans], 1, 1))
                above = jnp.where(lane == depth - 1, 0.0, pltpu.roll(part[2 * chans :], depth - 1, 1))
                emit(x, y + side, below + part[chans : 2 * chans] + above)
        return carry

    lax.fori_loop(0, wide - 2, body, 0)


def weights_kernel(one, two, w_pre, w_act, w_branch):
    chans = one.shape[-1]
    for kz in range(3):
        rows = slice(kz * chans, (kz + 1) * chans)
        taps = jnp.concatenate([one[a, b, kz] for a in range(3) for b in range(3)], axis=0)
        w_pre[rows] = taps.T
        for source, dest in ((two, w_act), (one, w_branch)):
            dest[rows] = jnp.concatenate(
                [source[2 - a, 2 - b, 2 - kz] for a in range(3) for b in range(3)], axis=1
            )


def forward_kernel(place, mask, weights, tile, xr_even, xr_odd, yr_even, yr_odd, activ, slope, padded):
    pad_tile(padded, place, tile, xr_even, xr_odd, yr_even, yr_odd, 0)

    def emit(x, y, value):
        sig = jax.nn.sigmoid(value)
        activ[x, y] = (mask[...] * (value * sig)).astype(BF16)
        slope[x, y] = mask[...] * (sig * (1.0 + value * (1.0 - sig)))

    conv_padded(padded, weights, 0, tile.shape[1], emit)


def backward_kernel(
    place, weights, slope, tile, xr_even, xr_odd, yr_even, yr_odd, pre_grad, xs_even, xs_odd, padded
):
    pad_tile(padded, place, tile, xr_even, xr_odd, yr_even, yr_odd, 1)
    size_x = tile.shape[0]

    def emit(x, y, value):
        pre_grad[x, y] = (slope[x, y] * value).astype(BF16)

    conv_padded(padded, weights, 0, tile.shape[1], emit)
    xs_even[0] = pre_grad[(1 - place[0]) * (size_x - 1)]
    xs_odd[0] = pre_grad[place[0] * (size_x - 1)]


def branch_part(mask, weights, base, padded, result, first):
    def emit(x, y, value):
        result[x, y - first] = (base[x, y].astype(F32) + mask[...] * value).astype(BF16)

    conv_padded(padded, weights, first, result.shape[1], emit)


def branch_low_kernel(place, mask, weights, base, tile, xr_even, xr_odd, yr_even, yr_odd, result, padded):
    pad_tile(padded, place, tile, xr_even, xr_odd, yr_even, yr_odd, 0)
    branch_part(mask, weights, base, padded, result, 0)


def branch_high_kernel(mask, weights, base, padded, result):
    branch_part(mask, weights, base, padded, result, base.shape[1] // 2)


def grad_accumulate(padded, stack, acc):
    size_x, size_y, _, _ = stack.shape
    acc[...] = jnp.zeros_like(acc)

    def body(i, carry):
        right = jnp.concatenate([stack[i, y] for y in range(size_y)], axis=1)
        left = []
        for a in range(3):
            rows = [padded[i + a, y] for y in range(size_y + 2)]
            for b in range(3):
                left.append(jnp.concatenate(rows[b : b + size_y], axis=1))
        left = jnp.concatenate(left, axis=0)
        acc[...] += lax.dot_general(left, right, (((1,), (1,)), ((), ())), preferred_element_type=F32)
        return carry

    lax.fori_loop(0, size_x, body, 0)


def pack_grad(dest, acc, chans):
    rows = acc.shape[0]
    half = rows // 2
    dest[0:rows] = acc[:, 0 : 2 * chans]
    low = acc[0:half, 2 * chans : 3 * chans]
    high = acc[half:rows, 2 * chans : 3 * chans]
    dest[rows : rows + half] = jnp.concatenate([low, high], axis=1)


def stack_tile(stack, source):
    def body(i, carry):
        stack_row(stack, i, 0, source[i])
        return carry

    lax.fori_loop(0, source.shape[0], body, 0)


def grad_two_kernel(grad_pad, activ, packed, stack, acc):
    stack_tile(stack, activ)
    grad_accumulate(grad_pad, stack, acc)
    pack_grad(packed, acc, activ.shape[2])


def grad_one_kernel(place, in_pad, pre_grad, packed_two, keep, send, stack, acc):
    stack_tile(stack, pre_grad)
    grad_accumulate(in_pad, stack, acc)

    @pl.when(place[0] == 0)
    def _():
        pack_grad(keep, acc, pre_grad.shape[2])
        send[...] = packed_two[...]

    @pl.when(place[0] != 0)
    def _():
        pack_grad(send, acc, pre_grad.shape[2])
        keep[...] = packed_two[...]


def split_kernel(place, keep, recv, *outs):
    rows = outs[0].shape[0]
    for dist, out in enumerate(outs):
        start = pl.multiple_of((place[2] ^ dist) * rows, 8)
        out[...] = keep[pl.ds(start, rows)] + recv[pl.ds(start, rows)]


def join_kernel(place, *refs):
    out = refs[-1]
    rows = refs[0].shape[0]
    for dist, part in enumerate(refs[:-1]):
        start = pl.multiple_of((place[2] ^ dist) * rows, 8)
        out[pl.ds(start, rows)] = part[...]


def unpack_kernel(place, scale, own, other, grad_one, grad_two):
    chans = grad_one.shape[-1]
    rows = 9 * chans
    half = rows // 2

    def block(source, a, b, j):
        start = (3 * a + b) * chans
        if j < 2:
            return source[start : start + chans, j * chans : (j + 1) * chans]
        pieces = []
        step = chans // 2
        for first in (start, start + step):
            if first < half:
                pieces.append(source[rows + first : rows + first + step, 0:chans])
            else:
                pieces.append(source[rows + first - half : rows + first - half + step, chans : 2 * chans])
        return jnp.concatenate(pieces, axis=0)

    def write(one, two):
        for a in range(3):
            for b in range(3):
                for j in range(3):
                    grad_one[a, b, 2 - j] = block(one, a, b, j) * scale
                    grad_two[2 - a, 2 - b, j] = block(two, a, b, j).T * scale

    @pl.when(place[0] == 0)
    def _():
        write(own, other)

    @pl.when(place[0] != 0)
    def _():
        write(other, own)


def call(kernel, outs, scratch=(), scalars=0, flops=0):
    def run(*operands):
        specs = [pl.BlockSpec(memory_space=pltpu.SMEM)] * scalars
        specs += [pl.BlockSpec(memory_space=pltpu.VMEM)] * (len(operands) - scalars)
        moved = sum(o.size * o.dtype.itemsize for o in operands)
        moved += sum(math.prod(o.shape) * o.dtype.itemsize for o in outs)
        return pl.pallas_call(
            kernel,
            out_shape=tuple(outs),
            in_specs=specs,
            out_specs=tuple(pl.BlockSpec(memory_space=pltpu.VMEM) for _ in outs),
            scratch_shapes=list(scratch),
            cost_estimate=pl.CostEstimate(flops=flops, bytes_accessed=moved, transcendentals=0),
            compiler_params=pltpu.CompilerParams(vmem_limit_bytes=40 * 1024 * 1024),
        )(*operands)

    return run


def body(features, cotangent, block_mask, kernel_one, kernel_two):
    chans, tile_x, tile_y, tile_z = features.shape
    blocks = block_mask.shape[2]
    cells_all = tile_x * tile_y * tile_z * lax.axis_size("gx") * lax.axis_size("gy")
    scale = 1.0 / math.sqrt(cells_all)
    place_x, place_y = lax.axis_index("gx"), lax.axis_index("gy")
    x_odd, y_odd = place_x & 1, place_y & 1
    place = jnp.stack([x_odd, y_odd, (place_x >> 1) & 3]).astype(jnp.int32)

    mask = jnp.broadcast_to(block_mask.reshape(blocks, 1), (blocks, tile_z // blocks)).reshape(1, tile_z)
    mask_f = mask.astype(F32)
    mask_b = mask.astype(BF16).reshape(1, 1, tile_z)

    def x_edges(at):
        both = [lax.dynamic_index_in_dim(a, at, 1, keepdims=False) * mask_b for a in (features, cotangent)]
        return jnp.stack([jnp.transpose(a, (1, 0, 2)) for a in both])

    xr = swap(x_edges((1 - x_odd) * (tile_x - 1)), x_edges(x_odd * (tile_x - 1)), "gx")
    masked_in = jnp.transpose(features * mask_b[:, None], (1, 2, 0, 3))
    masked_grad = jnp.transpose(cotangent * mask_b[:, None], (1, 2, 0, 3))

    tile_shape = (tile_x, tile_y, chans, tile_z)
    tile_b = jax.ShapeDtypeStruct(tile_shape, BF16)
    column_b = jax.ShapeDtypeStruct((tile_x + 2, chans, tile_z), BF16)
    edge_b = jax.ShapeDtypeStruct((1, tile_y, chans, tile_z), BF16)
    pad_b = jax.ShapeDtypeStruct((tile_x + 2, tile_y + 2, chans, tile_z), BF16)
    flops = 2 * 27 * chans * chans * tile_x * tile_y * tile_z

    def y_sends(tile, halo_x, which):
        kernel = functools.partial(ypack_kernel, which=which)
        return call(kernel, [column_b] * 2, scalars=1)(place, tile, *halo_x)

    in_sends = y_sends(masked_in, xr, 0)
    grad_sends = y_sends(masked_grad, xr, 1)
    matrix = jax.ShapeDtypeStruct((3 * chans, 9 * chans), BF16)
    even, odd = swap_perms(lax.axis_size("gy"))
    in_even = lax.ppermute(in_sends[0], "gy", even)
    w_pre, w_act, w_branch = call(weights_kernel, [matrix] * 3)(kernel_one, kernel_two)
    in_next, w_pre = lax.optimization_barrier((in_sends[1], w_pre))
    in_odd = lax.ppermute(in_next, "gy", odd)
    in_y = (in_even, in_odd)
    grad_y = swap(*grad_sends, "gy")

    tile_s = pltpu.VMEM((tile_x, tile_y, 3 * chans, tile_z), BF16)
    grad_s = pltpu.VMEM((9 * chans, 3 * chans), F32)

    activ, slope, in_pad = call(
        forward_kernel, [tile_b, jax.ShapeDtypeStruct(tile_shape, F32), pad_b], scalars=1, flops=flops
    )(place, mask_f, w_pre, masked_in, *xr, *in_y)
    pre_grad, xs_even, xs_odd, grad_pad = call(
        backward_kernel, [tile_b, edge_b, edge_b, pad_b], scalars=1, flops=flops
    )(place, w_act, slope, masked_grad, *xr, *grad_y)

    packed = 27 * chans * chans // (2 * chans)
    half = jax.ShapeDtypeStruct((packed, 2 * chans), F32)
    pre_xr = swap(xs_even, xs_odd, "gx")
    (packed_two,) = call(grad_two_kernel, [half], [tile_s, grad_s], flops=flops)(grad_pad, activ)
    pre_sends = y_sends(pre_grad, pre_xr, 0)
    pre_yr = swap(*pre_sends, "gy")
    keep, send = call(grad_one_kernel, [half, half], [tile_s, grad_s], scalars=1, flops=flops)(
        place, in_pad, pre_grad, packed_two
    )

    recv = xor_permute(send, 8)
    chunk = jax.ShapeDtypeStruct((packed // 4, 2 * chans), F32)
    parts = call(split_kernel, [chunk] * 4, scalars=1)(place, keep, recv)
    parts = [parts[0]] + [xor_permute(parts[d], 16 * d) for d in range(1, 4)]
    part = (parts[0] + parts[1]) + (parts[2] + parts[3])
    for masks in ((2, 4, 6), (1, 64, 65)):
        near, mid, far = [xor_permute(part, m) for m in masks]
        part = (part + near) + (mid + far)
    pieces = [part] + [xor_permute(part, 16 * d) for d in range(1, 4)]
    (own,) = call(join_kernel, [half], scalars=1)(place, *pieces)
    other = xor_permute(own, 8)
    grad_shape = jax.ShapeDtypeStruct((3, 3, 3, chans, chans), F32)

    def unpack(place_ref, own_ref, other_ref, one_ref, two_ref):
        unpack_kernel(place_ref, scale, own_ref, other_ref, one_ref, two_ref)

    grad_one, grad_two = call(unpack, [grad_shape, grad_shape], scalars=1)(place, own, other)

    half_b = jax.ShapeDtypeStruct((tile_x, tile_y // 2, chans, tile_z), BF16)
    low, pre_pad = call(
        branch_low_kernel, [half_b, pad_b], scalars=1, flops=flops // 2
    )(place, mask_f, w_branch, masked_grad, pre_grad, *pre_xr, *pre_yr)
    (high,) = call(branch_high_kernel, [half_b], flops=flops // 2)(mask_f, w_branch, masked_grad, pre_pad)
    grad_features = jnp.transpose(jnp.concatenate([low, high], axis=1), (2, 0, 1, 3))
    return grad_features, grad_one, grad_two


def solution(mesh):
    placed = (P(None, "gx", "gy", None), P(None, "gx", "gy", None), P("gx", "gy", None), P(), P())
    return jax.shard_map(
        body,
        mesh=mesh,
        in_specs=placed,
        out_specs=(P(None, "gx", "gy", None), P(), P()),
        check_vma=False,
    )
```

```python
import math

import jax
import jax.numpy as jnp
from jax import lax
from jax.experimental import pallas as pl
from jax.experimental.pallas import tpu as pltpu
from jax.sharding import PartitionSpec as P


F32 = jnp.float32
BF16 = jnp.bfloat16
AXES = ("gx", "gy")


def swap_perms(count):
    even = [(i, i ^ 1) for i in range(count)]
    odd = [(i, i + 1 if i % 2 else i - 1) for i in range(1, count - 1)]
    return even, odd


def xor_permute(value, mask):
    total = lax.axis_size("gx") * lax.axis_size("gy")
    return lax.ppermute(value, AXES, [(i, i ^ mask) for i in range(total)])


def swap(value_even, value_odd, axis):
    even, odd = swap_perms(lax.axis_size(axis))
    return lax.ppermute(value_even, axis, even), lax.ppermute(value_odd, axis, odd)


def store_shifted(stack, x, y, value):
    chans, depth = value.shape
    lane = lax.broadcasted_iota(jnp.int32, value.shape, 1)
    below = jnp.where(lane == 0, 0.0, pltpu.roll(value, 1, 1))
    above = jnp.where(lane == depth - 1, 0.0, pltpu.roll(value, depth - 1, 1))
    stack[x, y, 0:chans] = below.astype(BF16)
    stack[x, y, chans : 2 * chans] = value.astype(BF16)
    stack[x, y, 2 * chans : 3 * chans] = above.astype(BF16)


def sides(parity, size):
    even = (1 - parity) * (size + 1)
    return even, size + 1 - even


def pad_tile(padded, place, tile, xr_even, xr_odd, yr_even, yr_odd, which):
    size_x, size_y = tile.shape[0], tile.shape[1]
    x_even, x_odd = sides(place[0], size_x)
    y_even, y_odd = sides(place[1], size_y)
    padded[x_even, 1 : size_y + 1] = xr_even[which]
    padded[x_odd, 1 : size_y + 1] = xr_odd[which]
    for i in range(size_x + 2):
        padded[i, y_even] = yr_even[which, i]
        padded[i, y_odd] = yr_odd[which, i]

    def body(i, carry):
        padded[i + 1, 1 : size_y + 1] = tile[i]
        return carry

    lax.fori_loop(0, size_x, body, 0)


def ypack_kernel(place, ye_even, ye_odd, xr_even, xr_odd, ys_even, ys_odd):
    count, size_x = ye_even.shape[0:2]
    size_y = xr_even.shape[1]
    x_even, x_odd = sides(place[0], size_x)
    at_even, at_odd = (1 - place[1]) * (size_y - 1), place[1] * (size_y - 1)
    for out, edge, at in ((ys_even, ye_even, at_even), (ys_odd, ye_odd, at_odd)):
        for k in range(count):
            out[k, x_even] = xr_even[k, at]
            out[k, x_odd] = xr_odd[k, at]
            for i in range(size_x):
                out[k, i + 1] = edge[k, i]


def conv_padded(padded, weights, first, count, emit):
    wide, _, chans, depth = padded.shape

    def body(x, carry):
        lane = lax.broadcasted_iota(jnp.int32, (chans, depth), 1)
        for y in range(first, first + count, 2):
            halves = []
            for side in range(2):
                at = y + side
                rows = [padded[x + a, at : at + 3].reshape(3 * chans, depth) for a in range(3)]
                halves.append(jnp.concatenate(rows, axis=0))
            out = jnp.dot(weights[...], jnp.concatenate(halves, axis=1), preferred_element_type=F32)
            for side in range(2):
                part = out[:, side * depth : (side + 1) * depth]
                below = jnp.where(lane == 0, 0.0, pltpu.roll(part[0:chans], 1, 1))
                above = jnp.where(lane == depth - 1, 0.0, pltpu.roll(part[2 * chans :], depth - 1, 1))
                emit(x, y + side, below + part[chans : 2 * chans] + above)
        return carry

    lax.fori_loop(0, wide - 2, body, 0)


def weights_kernel(one, two, w_pre, w_act, w_branch):
    chans = one.shape[-1]
    for kz in range(3):
        rows = slice(kz * chans, (kz + 1) * chans)
        taps = jnp.concatenate([one[a, b, kz] for a in range(3) for b in range(3)], axis=0)
        w_pre[rows] = taps.T
        for source, dest in ((two, w_act), (one, w_branch)):
            dest[rows] = jnp.concatenate(
                [source[2 - a, 2 - b, 2 - kz] for a in range(3) for b in range(3)], axis=1
            )


def forward_kernel(place, mask, weights, tile, xr_even, xr_odd, yr_even, yr_odd, activ, slope, padded):
    pad_tile(padded, place, tile, xr_even, xr_odd, yr_even, yr_odd, 0)

    def emit(x, y, value):
        sig = jax.nn.sigmoid(value)
        store_shifted(activ, x, y, mask[...] * (value * sig))
        slope[x, y] = mask[...] * (sig * (1.0 + value * (1.0 - sig)))

    conv_padded(padded, weights, 0, tile.shape[1], emit)


def backward_kernel(
    place, weights, slope, tile, xr_even, xr_odd, yr_even, yr_odd,
    pre_grad, shifted, xs_even, xs_odd, ye_even, ye_odd, padded,
):
    pad_tile(padded, place, tile, xr_even, xr_odd, yr_even, yr_odd, 1)
    size_x = tile.shape[0]

    def emit(x, y, value):
        value = slope[x, y] * value
        pre_grad[x, y] = value.astype(BF16)
        store_shifted(shifted, x, y, value)

    conv_padded(padded, weights, 0, tile.shape[1], emit)
    last_y = tile.shape[1] - 1
    xs_even[0] = pre_grad[(1 - place[0]) * (size_x - 1)]
    xs_odd[0] = pre_grad[place[0] * (size_x - 1)]
    for i in range(size_x):
        ye_even[0, i] = pre_grad[i, (1 - place[1]) * last_y]
        ye_odd[0, i] = pre_grad[i, place[1] * last_y]


def branch_part(mask, weights, base, padded, result, first):
    def emit(x, y, value):
        result[x, y - first] = (base[x, y].astype(F32) + mask[...] * value).astype(BF16)

    conv_padded(padded, weights, first, result.shape[1], emit)


def branch_low_kernel(place, mask, weights, base, tile, xr_even, xr_odd, yr_even, yr_odd, result, padded):
    pad_tile(padded, place, tile, xr_even, xr_odd, yr_even, yr_odd, 0)
    branch_part(mask, weights, base, padded, result, 0)


def branch_high_kernel(mask, weights, base, padded, result):
    branch_part(mask, weights, base, padded, result, base.shape[1] // 2)


def grad_accumulate(padded, stack, acc):
    size_x, size_y, _, _ = stack.shape
    acc[...] = jnp.zeros_like(acc)

    def body(i, carry):
        right = jnp.concatenate([stack[i, y] for y in range(size_y)], axis=1)
        left = []
        for a in range(3):
            rows = [padded[i + a, y] for y in range(size_y + 2)]
            for b in range(3):
                left.append(jnp.concatenate(rows[b : b + size_y], axis=1))
        left = jnp.concatenate(left, axis=0)
        acc[...] += lax.dot_general(left, right, (((1,), (1,)), ((), ())), preferred_element_type=F32)
        return carry

    lax.fori_loop(0, size_x, body, 0)


def pack_grad(dest, acc, chans):
    rows = acc.shape[0]
    half = rows // 2
    dest[0:rows] = acc[:, 0 : 2 * chans]
    low = acc[0:half, 2 * chans : 3 * chans]
    high = acc[half:rows, 2 * chans : 3 * chans]
    dest[rows : rows + half] = jnp.concatenate([low, high], axis=1)


def grad_two_kernel(grad_pad, activ, packed, acc):
    grad_accumulate(grad_pad, activ, acc)
    pack_grad(packed, acc, grad_pad.shape[2])


def grad_one_kernel(place, in_pad, shifted, packed_two, keep, send, acc):
    grad_accumulate(in_pad, shifted, acc)

    @pl.when(place[0] == 0)
    def _():
        pack_grad(keep, acc, in_pad.shape[2])
        send[...] = packed_two[...]

    @pl.when(place[0] != 0)
    def _():
        pack_grad(send, acc, in_pad.shape[2])
        keep[...] = packed_two[...]


def split_kernel(place, keep, recv, *outs):
    rows = outs[0].shape[0]
    for dist, out in enumerate(outs):
        start = pl.multiple_of((place[2] ^ dist) * rows, 8)
        out[...] = keep[pl.ds(start, rows)] + recv[pl.ds(start, rows)]


def join_kernel(place, *refs):
    out = refs[-1]
    rows = refs[0].shape[0]
    for dist, part in enumerate(refs[:-1]):
        start = pl.multiple_of((place[2] ^ dist) * rows, 8)
        out[pl.ds(start, rows)] = part[...]


def unpack_kernel(place, scale, own, other, grad_one, grad_two):
    chans = grad_one.shape[-1]
    rows = 9 * chans
    half = rows // 2

    def block(source, a, b, j):
        start = (3 * a + b) * chans
        if j < 2:
            return source[start : start + chans, j * chans : (j + 1) * chans]
        pieces = []
        step = chans // 2
        for first in (start, start + step):
            if first < half:
                pieces.append(source[rows + first : rows + first + step, 0:chans])
            else:
                pieces.append(source[rows + first - half : rows + first - half + step, chans : 2 * chans])
        return jnp.concatenate(pieces, axis=0)

    def write(one, two):
        for a in range(3):
            for b in range(3):
                for j in range(3):
                    grad_one[a, b, 2 - j] = block(one, a, b, j) * scale
                    grad_two[2 - a, 2 - b, j] = block(two, a, b, j).T * scale

    @pl.when(place[0] == 0)
    def _():
        write(own, other)

    @pl.when(place[0] != 0)
    def _():
        write(other, own)


def call(kernel, outs, scratch=(), scalars=0, flops=0):
    def run(*operands):
        specs = [pl.BlockSpec(memory_space=pltpu.SMEM)] * scalars
        specs += [pl.BlockSpec(memory_space=pltpu.VMEM)] * (len(operands) - scalars)
        moved = sum(o.size * o.dtype.itemsize for o in operands)
        moved += sum(math.prod(o.shape) * o.dtype.itemsize for o in outs)
        return pl.pallas_call(
            kernel,
            out_shape=tuple(outs),
            in_specs=specs,
            out_specs=tuple(pl.BlockSpec(memory_space=pltpu.VMEM) for _ in outs),
            scratch_shapes=list(scratch),
            cost_estimate=pl.CostEstimate(flops=flops, bytes_accessed=moved, transcendentals=0),
            compiler_params=pltpu.CompilerParams(vmem_limit_bytes=40 * 1024 * 1024),
        )(*operands)

    return run


def body(features, cotangent, block_mask, kernel_one, kernel_two):
    chans, tile_x, tile_y, tile_z = features.shape
    blocks = block_mask.shape[2]
    cells_all = tile_x * tile_y * tile_z * lax.axis_size("gx") * lax.axis_size("gy")
    scale = 1.0 / math.sqrt(cells_all)
    place_x, place_y = lax.axis_index("gx"), lax.axis_index("gy")
    x_odd, y_odd = place_x & 1, place_y & 1
    place = jnp.stack([x_odd, y_odd, (place_x >> 1) & 3]).astype(jnp.int32)

    mask = jnp.broadcast_to(block_mask.reshape(blocks, 1), (blocks, tile_z // blocks)).reshape(1, tile_z)
    mask_f = mask.astype(F32)
    mask_b = mask.astype(BF16).reshape(1, 1, tile_z)

    def x_edges(at):
        both = [lax.dynamic_index_in_dim(a, at, 1, keepdims=False) * mask_b for a in (features, cotangent)]
        return jnp.stack([jnp.transpose(a, (1, 0, 2)) for a in both])

    def y_edges(at):
        both = [lax.dynamic_index_in_dim(a, at, 2, keepdims=False) * mask_b for a in (features, cotangent)]
        return jnp.stack([jnp.transpose(a, (1, 0, 2)) for a in both])

    ends = ((1 - x_odd) * (tile_x - 1), x_odd * (tile_x - 1)), ((1 - y_odd) * (tile_y - 1), y_odd * (tile_y - 1))
    xr = swap(x_edges(ends[0][0]), x_edges(ends[0][1]), "gx")
    even, odd = swap_perms(lax.axis_size("gy"))

    def columns(count):
        return [jax.ShapeDtypeStruct((count, tile_x + 2, chans, tile_z), BF16)] * 2

    sends = call(ypack_kernel, columns(2), scalars=1)(place, y_edges(ends[1][0]), y_edges(ends[1][1]), *xr)
    yr_even = lax.ppermute(sends[0], "gy", even)
    masked_in = jnp.transpose(features * mask_b[:, None], (1, 2, 0, 3))
    masked_grad = jnp.transpose(cotangent * mask_b[:, None], (1, 2, 0, 3))
    odd_send, masked_in, masked_grad = lax.optimization_barrier((sends[1], masked_in, masked_grad))
    yr_odd = lax.ppermute(odd_send, "gy", odd)

    tile_shape = (tile_x, tile_y, chans, tile_z)
    tile_b = jax.ShapeDtypeStruct(tile_shape, BF16)
    shifted_b = jax.ShapeDtypeStruct((tile_x, tile_y, 3 * chans, tile_z), BF16)
    edge_x = jax.ShapeDtypeStruct((1, tile_y, chans, tile_z), BF16)
    edge_y = jax.ShapeDtypeStruct((1, tile_x, chans, tile_z), BF16)
    pad_b = jax.ShapeDtypeStruct((tile_x + 2, tile_y + 2, chans, tile_z), BF16)
    matrix = jax.ShapeDtypeStruct((3 * chans, 9 * chans), BF16)
    grad_s = pltpu.VMEM((9 * chans, 3 * chans), F32)
    flops = 2 * 27 * chans * chans * tile_x * tile_y * tile_z

    w_pre, w_act, w_branch = call(weights_kernel, [matrix] * 3)(kernel_one, kernel_two)
    activ, slope, in_pad = call(
        forward_kernel, [shifted_b, jax.ShapeDtypeStruct(tile_shape, F32), pad_b], scalars=1, flops=flops
    )(place, mask_f, w_pre, masked_in, *xr, yr_even, yr_odd)
    pre_grad, shifted, xs_even, xs_odd, ye_even, ye_odd, grad_pad = call(
        backward_kernel, [tile_b, shifted_b, edge_x, edge_x, edge_y, edge_y, pad_b], scalars=1, flops=flops
    )(place, w_act, slope, masked_grad, *xr, yr_even, yr_odd)

    packed = 27 * chans * chans // (2 * chans)
    half = jax.ShapeDtypeStruct((packed, 2 * chans), F32)
    pre_xr = swap(xs_even, xs_odd, "gx")
    (packed_two,) = call(grad_two_kernel, [half], [grad_s], flops=flops)(grad_pad, activ)
    pre_sends = call(ypack_kernel, columns(1), scalars=1)(place, ye_even, ye_odd, *pre_xr)
    pre_even = lax.ppermute(pre_sends[0], "gy", even)
    keep, send = call(grad_one_kernel, [half, half], [grad_s], scalars=1, flops=flops)(
        place, in_pad, shifted, packed_two
    )
    pre_send, send = lax.optimization_barrier((pre_sends[1], send))
    pre_odd = lax.ppermute(pre_send, "gy", odd)
    pre_yr = (pre_even, pre_odd)

    recv = xor_permute(send, 8)
    chunk = jax.ShapeDtypeStruct((packed // 4, 2 * chans), F32)
    parts = call(split_kernel, [chunk] * 4, scalars=1)(place, keep, recv)
    parts = [parts[0]] + [xor_permute(parts[d], 16 * d) for d in range(1, 4)]
    part = (parts[0] + parts[1]) + (parts[2] + parts[3])
    for masks in ((2, 4, 6), (1, 64, 65)):
        near, mid, far = [xor_permute(part, m) for m in masks]
        part = (part + near) + (mid + far)
    pieces = [part] + [xor_permute(part, 16 * d) for d in range(1, 4)]
    (own,) = call(join_kernel, [half], scalars=1)(place, *pieces)
    other = xor_permute(own, 8)
    grad_shape = jax.ShapeDtypeStruct((3, 3, 3, chans, chans), F32)

    def unpack(place_ref, own_ref, other_ref, one_ref, two_ref):
        unpack_kernel(place_ref, scale, own_ref, other_ref, one_ref, two_ref)

    grad_one, grad_two = call(unpack, [grad_shape, grad_shape], scalars=1)(place, own, other)

    half_b = jax.ShapeDtypeStruct((tile_x, tile_y // 2, chans, tile_z), BF16)
    low, pre_pad = call(
        branch_low_kernel, [half_b, pad_b], scalars=1, flops=flops // 2
    )(place, mask_f, w_branch, masked_grad, pre_grad, *pre_xr, *pre_yr)
    (high,) = call(branch_high_kernel, [half_b], flops=flops // 2)(mask_f, w_branch, masked_grad, pre_pad)
    grad_features = jnp.transpose(jnp.concatenate([low, high], axis=1), (2, 0, 1, 3))
    return grad_features, grad_one, grad_two


def solution(mesh):
    placed = (P(None, "gx", "gy", None), P(None, "gx", "gy", None), P("gx", "gy", None), P(), P())
    return jax.shard_map(
        body,
        mesh=mesh,
        in_specs=placed,
        out_specs=(P(None, "gx", "gy", None), P(), P()),
        check_vma=False,
    )
```

```python
import math

import jax
import jax.numpy as jnp
from jax import lax
from jax.experimental import pallas as pl
from jax.experimental.pallas import tpu as pltpu
from jax.sharding import PartitionSpec as P


F32 = jnp.float32
BF16 = jnp.bfloat16
AXES = ("gx", "gy")


def swap_perms(count):
    even = [(i, i ^ 1) for i in range(count)]
    odd = [(i, i + 1 if i % 2 else i - 1) for i in range(1, count - 1)]
    return even, odd


def xor_permute(value, mask):
    total = lax.axis_size("gx") * lax.axis_size("gy")
    return lax.ppermute(value, AXES, [(i, i ^ mask) for i in range(total)])


def swap(value_even, value_odd, axis):
    even, odd = swap_perms(lax.axis_size(axis))
    return lax.ppermute(value_even, axis, even), lax.ppermute(value_odd, axis, odd)


def stack_row(stack, at_x, first_y, row):
    count, chans, depth = row.shape
    lane = lax.broadcasted_iota(jnp.int32, row.shape, 2)
    zero = jnp.zeros_like(row)
    below = jnp.where(lane == 0, zero, pltpu.roll(row, 1, 2))
    above = jnp.where(lane == depth - 1, zero, pltpu.roll(row, depth - 1, 2))
    ys = pl.ds(first_y, count)
    stack[at_x, ys, 0:chans, :] = below
    stack[at_x, ys, chans : 2 * chans, :] = row
    stack[at_x, ys, 2 * chans : 3 * chans, :] = above


def sides(parity, size):
    even = (1 - parity) * (size + 1)
    return even, size + 1 - even


def pad_tile(padded, place, tile, xr_even, xr_odd, yr_even, yr_odd, which):
    size_x, size_y = tile.shape[0], tile.shape[1]
    x_even, x_odd = sides(place[0], size_x)
    y_even, y_odd = sides(place[1], size_y)
    padded[x_even, 1 : size_y + 1] = xr_even[which]
    padded[x_odd, 1 : size_y + 1] = xr_odd[which]
    for i in range(size_x + 2):
        padded[i, y_even] = yr_even[i]
        padded[i, y_odd] = yr_odd[i]

    def body(i, carry):
        padded[i + 1, 1 : size_y + 1] = tile[i]
        return carry

    lax.fori_loop(0, size_x, body, 0)


def ypack_kernel(place, *refs):
    count = (len(refs) - 2) // 3
    tiles, (xr_even, xr_odd), outs = refs[:count], refs[count : count + 2], refs[count + 2 :]
    size_x, size_y = tiles[0].shape[0], tiles[0].shape[1]
    x_even, x_odd = sides(place[0], size_x)
    edges = (1 - place[1]) * (size_y - 1), place[1] * (size_y - 1)
    for k, tile in enumerate(tiles):
        for out, edge in zip(outs[2 * k : 2 * k + 2], edges):
            out[x_even] = xr_even[k, edge]
            out[x_odd] = xr_odd[k, edge]
            for i in range(size_x):
                out[i + 1] = tile[i, edge]


def conv_padded(padded, weights, first, count, emit):
    wide, _, chans, depth = padded.shape

    def body(x, carry):
        lane = lax.broadcasted_iota(jnp.int32, (chans, depth), 1)
        for y in range(first, first + count, 2):
            halves = []
            for side in range(2):
                at = y + side
                rows = [padded[x + a, at : at + 3].reshape(3 * chans, depth) for a in range(3)]
                halves.append(jnp.concatenate(rows, axis=0))
            out = jnp.dot(weights[...], jnp.concatenate(halves, axis=1), preferred_element_type=F32)
            for side in range(2):
                part = out[:, side * depth : (side + 1) * depth]
                below = jnp.where(lane == 0, 0.0, pltpu.roll(part[0:chans], 1, 1))
                above = jnp.where(lane == depth - 1, 0.0, pltpu.roll(part[2 * chans :], depth - 1, 1))
                emit(x, y + side, below + part[chans : 2 * chans] + above)
        return carry

    lax.fori_loop(0, wide - 2, body, 0)


def weights_kernel(one, two, w_pre, w_act, w_branch):
    chans = one.shape[-1]
    for kz in range(3):
        rows = slice(kz * chans, (kz + 1) * chans)
        taps = jnp.concatenate([one[a, b, kz] for a in range(3) for b in range(3)], axis=0)
        w_pre[rows] = taps.T
        for source, dest in ((two, w_act), (one, w_branch)):
            dest[rows] = jnp.concatenate(
                [source[2 - a, 2 - b, 2 - kz] for a in range(3) for b in range(3)], axis=1
            )


def forward_kernel(place, mask, weights, tile, xr_even, xr_odd, yr_even, yr_odd, activ, slope, padded):
    pad_tile(padded, place, tile, xr_even, xr_odd, yr_even, yr_odd, 0)

    def emit(x, y, value):
        sig = jax.nn.sigmoid(value)
        activ[x, y] = (mask[...] * (value * sig)).astype(BF16)
        slope[x, y] = mask[...] * (sig * (1.0 + value * (1.0 - sig)))

    conv_padded(padded, weights, 0, tile.shape[1], emit)


def backward_kernel(
    place, weights, slope, tile, xr_even, xr_odd, yr_even, yr_odd, pre_grad, xs_even, xs_odd, padded
):
    pad_tile(padded, place, tile, xr_even, xr_odd, yr_even, yr_odd, 1)
    size_x = tile.shape[0]

    def emit(x, y, value):
        pre_grad[x, y] = (slope[x, y] * value).astype(BF16)

    conv_padded(padded, weights, 0, tile.shape[1], emit)
    xs_even[0] = pre_grad[(1 - place[0]) * (size_x - 1)]
    xs_odd[0] = pre_grad[place[0] * (size_x - 1)]


def branch_part(mask, weights, base, padded, result, first):
    def emit(x, y, value):
        result[x, y - first] = (base[x, y].astype(F32) + mask[...] * value).astype(BF16)

    conv_padded(padded, weights, first, result.shape[1], emit)


def branch_low_kernel(place, mask, weights, base, tile, xr_even, xr_odd, yr_even, yr_odd, result, padded):
    pad_tile(padded, place, tile, xr_even, xr_odd, yr_even, yr_odd, 0)
    branch_part(mask, weights, base, padded, result, 0)


def branch_high_kernel(mask, weights, base, padded, result):
    branch_part(mask, weights, base, padded, result, base.shape[1] // 2)


def grad_accumulate(padded, stack, acc):
    size_x, size_y, _, _ = stack.shape
    acc[...] = jnp.zeros_like(acc)

    def body(i, carry):
        right = jnp.concatenate([stack[i, y] for y in range(size_y)], axis=1)
        left = []
        for a in range(3):
            rows = [padded[i + a, y] for y in range(size_y + 2)]
            for b in range(3):
                left.append(jnp.concatenate(rows[b : b + size_y], axis=1))
        left = jnp.concatenate(left, axis=0)
        acc[...] += lax.dot_general(left, right, (((1,), (1,)), ((), ())), preferred_element_type=F32)
        return carry

    lax.fori_loop(0, size_x, body, 0)


def pack_grad(dest, acc, chans):
    rows = acc.shape[0]
    half = rows // 2
    dest[0:rows] = acc[:, 0 : 2 * chans]
    low = acc[0:half, 2 * chans : 3 * chans]
    high = acc[half:rows, 2 * chans : 3 * chans]
    dest[rows : rows + half] = jnp.concatenate([low, high], axis=1)


def stack_tile(stack, source):
    def body(i, carry):
        stack_row(stack, i, 0, source[i])
        return carry

    lax.fori_loop(0, source.shape[0], body, 0)


def grad_two_kernel(grad_pad, activ, packed, stack, acc):
    stack_tile(stack, activ)
    grad_accumulate(grad_pad, stack, acc)
    pack_grad(packed, acc, activ.shape[2])


def grad_one_kernel(place, in_pad, pre_grad, packed_two, keep, send, stack, acc):
    stack_tile(stack, pre_grad)
    grad_accumulate(in_pad, stack, acc)

    @pl.when(place[0] == 0)
    def _():
        pack_grad(keep, acc, pre_grad.shape[2])
        send[...] = packed_two[...]

    @pl.when(place[0] != 0)
    def _():
        pack_grad(send, acc, pre_grad.shape[2])
        keep[...] = packed_two[...]


def split_kernel(place, keep, recv, *outs):
    rows = outs[0].shape[0]
    for dist, out in enumerate(outs):
        start = pl.multiple_of((place[2] ^ dist) * rows, 8)
        out[...] = keep[pl.ds(start, rows)] + recv[pl.ds(start, rows)]


def join_kernel(place, *refs):
    out = refs[-1]
    rows = refs[0].shape[0]
    for dist, part in enumerate(refs[:-1]):
        start = pl.multiple_of((place[2] ^ dist) * rows, 8)
        out[pl.ds(start, rows)] = part[...]


def unpack_kernel(place, scale, own, other, grad_one, grad_two):
    chans = grad_one.shape[-1]
    rows = 9 * chans
    half = rows // 2

    def block(source, a, b, j):
        start = (3 * a + b) * chans
        if j < 2:
            return source[start : start + chans, j * chans : (j + 1) * chans]
        pieces = []
        step = chans // 2
        for first in (start, start + step):
            if first < half:
                pieces.append(source[rows + first : rows + first + step, 0:chans])
            else:
                pieces.append(source[rows + first - half : rows + first - half + step, chans : 2 * chans])
        return jnp.concatenate(pieces, axis=0)

    def write(one, two):
        for a in range(3):
            for b in range(3):
                for j in range(3):
                    grad_one[a, b, 2 - j] = block(one, a, b, j) * scale
                start = (3 * a + b) * chans
                pair = two[start : start + chans, :].T * scale
                grad_two[2 - a, 2 - b, 0] = pair[0:chans]
                grad_two[2 - a, 2 - b, 1] = pair[chans : 2 * chans]
                grad_two[2 - a, 2 - b, 2] = block(two, a, b, 2).T * scale

    @pl.when(place[0] == 0)
    def _():
        write(own, other)

    @pl.when(place[0] != 0)
    def _():
        write(other, own)


def call(kernel, outs, scratch=(), scalars=0, flops=0):
    def run(*operands):
        specs = [pl.BlockSpec(memory_space=pltpu.SMEM)] * scalars
        specs += [pl.BlockSpec(memory_space=pltpu.VMEM)] * (len(operands) - scalars)
        moved = sum(o.size * o.dtype.itemsize for o in operands)
        moved += sum(math.prod(o.shape) * o.dtype.itemsize for o in outs)
        return pl.pallas_call(
            kernel,
            out_shape=tuple(outs),
            in_specs=specs,
            out_specs=tuple(pl.BlockSpec(memory_space=pltpu.VMEM) for _ in outs),
            scratch_shapes=list(scratch),
            cost_estimate=pl.CostEstimate(flops=flops, bytes_accessed=moved, transcendentals=0),
            compiler_params=pltpu.CompilerParams(vmem_limit_bytes=40 * 1024 * 1024),
        )(*operands)

    return run


def body(features, cotangent, block_mask, kernel_one, kernel_two):
    chans, tile_x, tile_y, tile_z = features.shape
    blocks = block_mask.shape[2]
    cells_all = tile_x * tile_y * tile_z * lax.axis_size("gx") * lax.axis_size("gy")
    scale = 1.0 / math.sqrt(cells_all)
    place_x, place_y = lax.axis_index("gx"), lax.axis_index("gy")
    x_odd, y_odd = place_x & 1, place_y & 1
    place = jnp.stack([x_odd, y_odd, (place_x >> 1) & 3]).astype(jnp.int32)

    mask = jnp.broadcast_to(block_mask.reshape(blocks, 1), (blocks, tile_z // blocks)).reshape(1, tile_z)
    mask_f = mask.astype(F32)
    mask_b = mask.astype(BF16).reshape(1, 1, tile_z)

    def x_edges(at):
        both = [lax.dynamic_index_in_dim(a, at, 1, keepdims=False) * mask_b for a in (features, cotangent)]
        return jnp.stack([jnp.transpose(a, (1, 0, 2)) for a in both])

    xr = swap(x_edges((1 - x_odd) * (tile_x - 1)), x_edges(x_odd * (tile_x - 1)), "gx")
    masked_in = jnp.transpose(features * mask_b[:, None], (1, 2, 0, 3))
    masked_grad = jnp.transpose(cotangent * mask_b[:, None], (1, 2, 0, 3))

    tile_shape = (tile_x, tile_y, chans, tile_z)
    tile_b = jax.ShapeDtypeStruct(tile_shape, BF16)
    column_b = jax.ShapeDtypeStruct((tile_x + 2, chans, tile_z), BF16)
    edge_b = jax.ShapeDtypeStruct((1, tile_y, chans, tile_z), BF16)
    pad_b = jax.ShapeDtypeStruct((tile_x + 2, tile_y + 2, chans, tile_z), BF16)
    flops = 2 * 27 * chans * chans * tile_x * tile_y * tile_z

    def y_sends(tiles, halo_x):
        outs = [column_b] * (2 * len(tiles))
        return call(ypack_kernel, outs, scalars=1)(place, *tiles, *halo_x)

    sends = y_sends((masked_in, masked_grad), xr)
    in_sends, grad_sends = sends[:2], sends[2:]
    matrix = jax.ShapeDtypeStruct((3 * chans, 9 * chans), BF16)
    even, odd = swap_perms(lax.axis_size("gy"))
    in_even = lax.ppermute(in_sends[0], "gy", even)
    w_pre, w_act, w_branch = call(weights_kernel, [matrix] * 3)(kernel_one, kernel_two)
    in_next, w_pre = lax.optimization_barrier((in_sends[1], w_pre))
    in_odd = lax.ppermute(in_next, "gy", odd)
    in_y = (in_even, in_odd)
    grad_y = swap(*grad_sends, "gy")

    tile_s = pltpu.VMEM((tile_x, tile_y, 3 * chans, tile_z), BF16)
    grad_s = pltpu.VMEM((9 * chans, 3 * chans), F32)

    activ, slope, in_pad = call(
        forward_kernel, [tile_b, jax.ShapeDtypeStruct(tile_shape, F32), pad_b], scalars=1, flops=flops
    )(place, mask_f, w_pre, masked_in, *xr, *in_y)
    pre_grad, xs_even, xs_odd, grad_pad = call(
        backward_kernel, [tile_b, edge_b, edge_b, pad_b], scalars=1, flops=flops
    )(place, w_act, slope, masked_grad, *xr, *grad_y)

    packed = 27 * chans * chans // (2 * chans)
    half = jax.ShapeDtypeStruct((packed, 2 * chans), F32)
    pre_xr = swap(xs_even, xs_odd, "gx")
    (packed_two,) = call(grad_two_kernel, [half], [tile_s, grad_s], flops=flops)(grad_pad, activ)
    pre_sends = y_sends((pre_grad,), pre_xr)
    pre_even = lax.ppermute(pre_sends[0], "gy", even)
    pre_odd = lax.ppermute(pre_sends[1], "gy", odd)
    pre_yr = (pre_even, pre_odd)
    keep, send = call(grad_one_kernel, [half, half], [tile_s, grad_s], scalars=1, flops=flops)(
        place, in_pad, pre_grad, packed_two
    )

    recv = xor_permute(send, 8)
    chunk = jax.ShapeDtypeStruct((packed // 4, 2 * chans), F32)
    parts = call(split_kernel, [chunk] * 4, scalars=1)(place, keep, recv)
    parts = [parts[0]] + [xor_permute(parts[d], 16 * d) for d in range(1, 4)]
    part = (parts[0] + parts[1]) + (parts[2] + parts[3])
    for masks in ((2, 4, 6), (1, 64, 65)):
        near, mid, far = [xor_permute(part, m) for m in masks]
        part = (part + near) + (mid + far)
    pieces = [part] + [xor_permute(part, 16 * d) for d in range(1, 4)]
    (own,) = call(join_kernel, [half], scalars=1)(place, *pieces)
    other = xor_permute(own, 8)
    grad_shape = jax.ShapeDtypeStruct((3, 3, 3, chans, chans), F32)

    def unpack(place_ref, own_ref, other_ref, one_ref, two_ref):
        unpack_kernel(place_ref, scale, own_ref, other_ref, one_ref, two_ref)

    grad_one, grad_two = call(unpack, [grad_shape, grad_shape], scalars=1)(place, own, other)

    half_b = jax.ShapeDtypeStruct((tile_x, tile_y // 2, chans, tile_z), BF16)
    low, pre_pad = call(
        branch_low_kernel, [half_b, pad_b], scalars=1, flops=flops // 2
    )(place, mask_f, w_branch, masked_grad, pre_grad, *pre_xr, *pre_yr)
    (high,) = call(branch_high_kernel, [half_b], flops=flops // 2)(mask_f, w_branch, masked_grad, pre_pad)
    grad_features = jnp.transpose(jnp.concatenate([low, high], axis=1), (2, 0, 1, 3))
    return grad_features, grad_one, grad_two


def solution(mesh):
    placed = (P(None, "gx", "gy", None), P(None, "gx", "gy", None), P("gx", "gy", None), P(), P())
    return jax.shard_map(
        body,
        mesh=mesh,
        in_specs=placed,
        out_specs=(P(None, "gx", "gy", None), P(), P()),
        check_vma=False,
    )
```

```python
import functools
import math

import jax
import jax.numpy as jnp
from jax import lax
from jax.experimental import pallas as pl
from jax.experimental.pallas import tpu as pltpu
from jax.sharding import PartitionSpec as P


F32 = jnp.float32
BF16 = jnp.bfloat16
AXES = ("gx", "gy")


def swap_perms(count):
    even = [(i, i ^ 1) for i in range(count)]
    odd = [(i, i + 1 if i % 2 else i - 1) for i in range(1, count - 1)]
    return even, odd


def xor_permute(value, mask):
    total = lax.axis_size("gx") * lax.axis_size("gy")
    return lax.ppermute(value, AXES, [(i, i ^ mask) for i in range(total)])


def swap(value_even, value_odd, axis):
    even, odd = swap_perms(lax.axis_size(axis))
    return lax.ppermute(value_even, axis, even), lax.ppermute(value_odd, axis, odd)


def stack_row(stack, at_x, first_y, row):
    count, chans, depth = row.shape
    lane = lax.broadcasted_iota(jnp.int32, row.shape, 2)
    zero = jnp.zeros_like(row)
    below = jnp.where(lane == 0, zero, pltpu.roll(row, 1, 2))
    above = jnp.where(lane == depth - 1, zero, pltpu.roll(row, depth - 1, 2))
    ys = pl.ds(first_y, count)
    stack[at_x, ys, 0:chans, :] = below
    stack[at_x, ys, chans : 2 * chans, :] = row
    stack[at_x, ys, 2 * chans : 3 * chans, :] = above


def sides(parity, size):
    even = (1 - parity) * (size + 1)
    return even, size + 1 - even


def pad_tile(padded, place, tile, xr_even, xr_odd, yr_even, yr_odd, which):
    size_x, size_y = tile.shape[0], tile.shape[1]
    x_even, x_odd = sides(place[0], size_x)
    y_even, y_odd = sides(place[1], size_y)
    padded[x_even, 1 : size_y + 1] = xr_even[which]
    padded[x_odd, 1 : size_y + 1] = xr_odd[which]
    for i in range(size_x + 2):
        padded[i, y_even] = yr_even[i]
        padded[i, y_odd] = yr_odd[i]

    def body(i, carry):
        padded[i + 1, 1 : size_y + 1] = tile[i]
        return carry

    lax.fori_loop(0, size_x, body, 0)


def ypack_kernel(place, *refs):
    count = (len(refs) - 2) // 3
    tiles, (xr_even, xr_odd), outs = refs[:count], refs[count : count + 2], refs[count + 2 :]
    size_x, size_y = tiles[0].shape[0], tiles[0].shape[1]
    x_even, x_odd = sides(place[0], size_x)
    edges = (1 - place[1]) * (size_y - 1), place[1] * (size_y - 1)
    for k, tile in enumerate(tiles):
        for out, edge in zip(outs[2 * k : 2 * k + 2], edges):
            out[x_even] = xr_even[k, edge]
            out[x_odd] = xr_odd[k, edge]
            for i in range(size_x):
                out[i + 1] = tile[i, edge]


def conv_padded(padded, weights, first, count, emit):
    wide, _, chans, depth = padded.shape

    def body(x, carry):
        lane = lax.broadcasted_iota(jnp.int32, (chans, depth), 1)
        for y in range(first, first + count, 2):
            halves = []
            for side in range(2):
                at = y + side
                rows = [padded[x + a, at : at + 3].reshape(3 * chans, depth) for a in range(3)]
                halves.append(jnp.concatenate(rows, axis=0))
            out = jnp.dot(weights[...], jnp.concatenate(halves, axis=1), preferred_element_type=F32)
            for side in range(2):
                part = out[:, side * depth : (side + 1) * depth]
                below = jnp.where(lane == 0, 0.0, pltpu.roll(part[0:chans], 1, 1))
                above = jnp.where(lane == depth - 1, 0.0, pltpu.roll(part[2 * chans :], depth - 1, 1))
                emit(x, y + side, below + part[chans : 2 * chans] + above)
        return carry

    lax.fori_loop(0, wide - 2, body, 0)


def weights_kernel(one, two, w_pre, w_act, w_branch):
    chans = one.shape[-1]
    for kz in range(3):
        rows = slice(kz * chans, (kz + 1) * chans)
        taps = jnp.concatenate([one[a, b, kz] for a in range(3) for b in range(3)], axis=0)
        w_pre[rows] = taps.T
        for source, dest in ((two, w_act), (one, w_branch)):
            dest[rows] = jnp.concatenate(
                [source[2 - a, 2 - b, 2 - kz] for a in range(3) for b in range(3)], axis=1
            )


def forward_kernel(place, mask, weights, tile, xr_even, xr_odd, yr_even, yr_odd, activ, slope, padded):
    pad_tile(padded, place, tile, xr_even, xr_odd, yr_even, yr_odd, 0)

    def emit(x, y, value):
        sig = jax.nn.sigmoid(value)
        activ[x, y] = (mask[...] * (value * sig)).astype(BF16)
        slope[x, y] = mask[...] * (sig * (1.0 + value * (1.0 - sig)))

    conv_padded(padded, weights, 0, tile.shape[1], emit)


def backward_kernel(
    place, weights, slope, tile, xr_even, xr_odd, yr_even, yr_odd, pre_grad, xs_even, xs_odd, padded
):
    pad_tile(padded, place, tile, xr_even, xr_odd, yr_even, yr_odd, 0)
    size_x = tile.shape[0]

    def emit(x, y, value):
        pre_grad[x, y] = (slope[x, y] * value).astype(BF16)

    conv_padded(padded, weights, 0, tile.shape[1], emit)
    xs_even[0] = pre_grad[(1 - place[0]) * (size_x - 1)]
    xs_odd[0] = pre_grad[place[0] * (size_x - 1)]


def branch_part(mask, weights, base, padded, result, first):
    def emit(x, y, value):
        result[x, y - first] = (base[x, y].astype(F32) + mask[...] * value).astype(BF16)

    conv_padded(padded, weights, first, result.shape[1], emit)


def branch_low_kernel(place, mask, weights, base, tile, xr_even, xr_odd, yr_even, yr_odd, result, padded):
    pad_tile(padded, place, tile, xr_even, xr_odd, yr_even, yr_odd, 0)
    branch_part(mask, weights, base, padded, result, 0)


def branch_high_kernel(mask, weights, base, padded, result):
    branch_part(mask, weights, base, padded, result, base.shape[1] // 2)


def grad_accumulate(padded, stack, acc):
    size_x, size_y, _, _ = stack.shape
    acc[...] = jnp.zeros_like(acc)

    def body(i, carry):
        right = jnp.concatenate([stack[i, y] for y in range(size_y)], axis=1)
        left = []
        for a in range(3):
            rows = [padded[i + a, y] for y in range(size_y + 2)]
            for b in range(3):
                left.append(jnp.concatenate(rows[b : b + size_y], axis=1))
        left = jnp.concatenate(left, axis=0)
        acc[...] += lax.dot_general(left, right, (((1,), (1,)), ((), ())), preferred_element_type=F32)
        return carry

    lax.fori_loop(0, size_x, body, 0)


def pack_grad(dest, acc, chans):
    rows = acc.shape[0]
    half = rows // 2
    dest[0:rows] = acc[:, 0 : 2 * chans]
    low = acc[0:half, 2 * chans : 3 * chans]
    high = acc[half:rows, 2 * chans : 3 * chans]
    dest[rows : rows + half] = jnp.concatenate([low, high], axis=1)


def stack_tile(stack, source):
    def body(i, carry):
        stack_row(stack, i, 0, source[i])
        return carry

    lax.fori_loop(0, source.shape[0], body, 0)


def grad_two_kernel(grad_pad, activ, packed, stack, acc):
    stack_tile(stack, activ)
    grad_accumulate(grad_pad, stack, acc)
    pack_grad(packed, acc, activ.shape[2])


def grad_one_kernel(place, in_pad, pre_grad, packed_two, keep, send, stack, acc):
    stack_tile(stack, pre_grad)
    grad_accumulate(in_pad, stack, acc)

    @pl.when(place[0] == 0)
    def _():
        pack_grad(keep, acc, pre_grad.shape[2])
        send[...] = packed_two[...]

    @pl.when(place[0] != 0)
    def _():
        pack_grad(send, acc, pre_grad.shape[2])
        keep[...] = packed_two[...]


def split_kernel(place, keep, recv, *outs):
    rows = outs[0].shape[0]
    for dist, out in enumerate(outs):
        start = pl.multiple_of((place[2] ^ dist) * rows, 8)
        out[...] = keep[pl.ds(start, rows)] + recv[pl.ds(start, rows)]


def join_kernel(place, *refs):
    out = refs[-1]
    rows = refs[0].shape[0]
    for dist, part in enumerate(refs[:-1]):
        start = pl.multiple_of((place[2] ^ dist) * rows, 8)
        out[pl.ds(start, rows)] = part[...]


def unpack(scale, source, dest, second):
    chans = dest.shape[-1]
    rows = 9 * chans
    half, step = rows // 2, chans // 2
    for a in range(3):
        for b in range(3):
            start = (3 * a + b) * chans
            both = source[start : start + chans, :] * scale
            pieces = []
            for first in (start, start + step):
                if first < half:
                    pieces.append(source[rows + first : rows + first + step, 0:chans])
                else:
                    pieces.append(source[rows + first - half : rows + first - half + step, chans : 2 * chans])
            tail = jnp.concatenate(pieces, axis=0) * scale
            if second:
                both = both.T
                dest[2 - a, 2 - b, 0] = both[0:chans]
                dest[2 - a, 2 - b, 1] = both[chans : 2 * chans]
                dest[2 - a, 2 - b, 2] = tail.T
            else:
                dest[a, b, 2] = both[:, 0:chans]
                dest[a, b, 1] = both[:, chans : 2 * chans]
                dest[a, b, 0] = tail


def unpack_own_kernel(place, own, dest, *, scale):
    @pl.when(place[0] == 0)
    def _():
        unpack(scale, own, dest, False)

    @pl.when(place[0] != 0)
    def _():
        unpack(scale, own, dest, True)


def unpack_other_kernel(place, mine, other, grad_one, grad_two, held, sems, *, scale):
    def finish(own_dest, other_dest, second):
        first = pltpu.make_async_copy(mine, own_dest, sems.at[0])
        first.start()
        unpack(scale, other, held, second)
        last = pltpu.make_async_copy(held, other_dest, sems.at[1])
        last.start()
        first.wait()
        last.wait()

    @pl.when(place[0] == 0)
    def _():
        finish(grad_one, grad_two, True)

    @pl.when(place[0] != 0)
    def _():
        finish(grad_two, grad_one, False)


def call(kernel, outs, scratch=(), scalars=0, flops=0, inside=True):
    def wrapped(*refs):
        if scalars:
            kernel([ref[0] for ref in refs[:scalars]], *refs[scalars:])
        else:
            kernel(*refs)

    def run(*operands):
        specs = [pl.BlockSpec(memory_space=pltpu.SMEM)] * scalars
        specs += [pl.BlockSpec(memory_space=pltpu.VMEM)] * (len(operands) - scalars)
        moved = sum(o.size * o.dtype.itemsize for o in operands)
        moved += sum(math.prod(o.shape) * o.dtype.itemsize for o in outs)
        return pl.pallas_call(
            wrapped,
            out_shape=tuple(outs),
            in_specs=specs,
            out_specs=tuple(pl.BlockSpec(memory_space=pltpu.VMEM if inside else pl.ANY) for _ in outs),
            scratch_shapes=list(scratch),
            cost_estimate=pl.CostEstimate(flops=flops, bytes_accessed=moved, transcendentals=0),
            compiler_params=pltpu.CompilerParams(vmem_limit_bytes=40 * 1024 * 1024),
        )(*operands)

    return run


def body(features, cotangent, block_mask, kernel_one, kernel_two):
    chans, tile_x, tile_y, tile_z = features.shape
    blocks = block_mask.shape[2]
    cells_all = tile_x * tile_y * tile_z * lax.axis_size("gx") * lax.axis_size("gy")
    scale = 1.0 / math.sqrt(cells_all)
    place_x, place_y = lax.axis_index("gx"), lax.axis_index("gy")
    x_odd, y_odd = place_x & 1, place_y & 1
    place = [v.astype(jnp.int32).reshape(1) for v in (x_odd, y_odd, (place_x >> 1) & 3)]

    mask = jnp.broadcast_to(block_mask.reshape(blocks, 1), (blocks, tile_z // blocks)).reshape(1, tile_z)
    mask_f = mask.astype(F32)
    mask_b = mask.astype(BF16).reshape(1, 1, tile_z)

    def x_swap(array):
        def edge(at):
            plane = lax.dynamic_index_in_dim(array, at, 1, keepdims=False) * mask_b
            return jnp.transpose(plane, (1, 0, 2))[None]

        return swap(edge((1 - x_odd) * (tile_x - 1)), edge(x_odd * (tile_x - 1)), "gx")

    in_xr = x_swap(features)
    masked_in = jnp.transpose(features * mask_b[:, None], (1, 2, 0, 3))

    tile_shape = (tile_x, tile_y, chans, tile_z)
    tile_b = jax.ShapeDtypeStruct(tile_shape, BF16)
    column_b = jax.ShapeDtypeStruct((tile_x + 2, chans, tile_z), BF16)
    edge_b = jax.ShapeDtypeStruct((1, tile_y, chans, tile_z), BF16)
    pad_b = jax.ShapeDtypeStruct((tile_x + 2, tile_y + 2, chans, tile_z), BF16)
    flops = 2 * 27 * chans * chans * tile_x * tile_y * tile_z

    def y_sends(tiles, halo_x):
        outs = [column_b] * (2 * len(tiles))
        return call(ypack_kernel, outs, scalars=3)(*place, *tiles, *halo_x)

    in_sends = y_sends((masked_in,), in_xr)
    matrix = jax.ShapeDtypeStruct((3 * chans, 9 * chans), BF16)
    even, odd = swap_perms(lax.axis_size("gy"))
    in_send, cotangent = lax.optimization_barrier((in_sends[0], cotangent))
    in_even = lax.ppermute(in_send, "gy", even)
    grad_xr = x_swap(cotangent)
    masked_grad = jnp.transpose(cotangent * mask_b[:, None], (1, 2, 0, 3))
    in_send, masked_grad = lax.optimization_barrier((in_sends[1], masked_grad))
    in_odd = lax.ppermute(in_send, "gy", odd)
    in_y = (in_even, in_odd)
    grad_sends = y_sends((masked_grad,), grad_xr)
    grad_even = lax.ppermute(grad_sends[0], "gy", even)
    w_pre, w_act, w_branch = call(weights_kernel, [matrix] * 3)(kernel_one, kernel_two)
    grad_send, w_pre = lax.optimization_barrier((grad_sends[1], w_pre))
    grad_odd = lax.ppermute(grad_send, "gy", odd)
    grad_y = (grad_even, grad_odd)

    tile_s = pltpu.VMEM((tile_x, tile_y, 3 * chans, tile_z), BF16)
    grad_s = pltpu.VMEM((9 * chans, 3 * chans), F32)

    activ, slope, in_pad = call(
        forward_kernel, [tile_b, jax.ShapeDtypeStruct(tile_shape, F32), pad_b], scalars=3, flops=flops
    )(*place, mask_f, w_pre, masked_in, *in_xr, *in_y)
    pre_grad, xs_even, xs_odd, grad_pad = call(
        backward_kernel, [tile_b, edge_b, edge_b, pad_b], scalars=3, flops=flops
    )(*place, w_act, slope, masked_grad, *grad_xr, *grad_y)

    packed = 27 * chans * chans // (2 * chans)
    half = jax.ShapeDtypeStruct((packed, 2 * chans), F32)
    pre_xr = swap(xs_even, xs_odd, "gx")
    (packed_two,) = call(grad_two_kernel, [half], [tile_s, grad_s], flops=flops)(grad_pad, activ)
    pre_sends = y_sends((pre_grad,), pre_xr)
    pre_even = lax.ppermute(pre_sends[0], "gy", even)
    pre_odd = lax.ppermute(pre_sends[1], "gy", odd)
    pre_yr = (pre_even, pre_odd)
    keep, send = call(grad_one_kernel, [half, half], [tile_s, grad_s], scalars=3, flops=flops)(
        *place, in_pad, pre_grad, packed_two
    )

    recv = xor_permute(send, 8)
    chunk = jax.ShapeDtypeStruct((packed // 4, 2 * chans), F32)
    parts = call(split_kernel, [chunk] * 4, scalars=3)(*place, keep, recv)
    parts = [parts[0]] + [xor_permute(parts[d], 16 * d) for d in range(1, 4)]
    part = (parts[0] + parts[1]) + (parts[2] + parts[3])
    for masks in ((2, 4, 6), (1, 64, 65)):
        near, mid, far = [xor_permute(part, m) for m in masks]
        part = (part + near) + (mid + far)
    pieces = [part] + [xor_permute(part, 16 * d) for d in range(1, 4)]
    (own,) = call(join_kernel, [half], scalars=3)(*place, *pieces)
    other = xor_permute(own, 8)
    grad_shape = jax.ShapeDtypeStruct((3, 3, 3, chans, chans), F32)

    (mine,) = call(functools.partial(unpack_own_kernel, scale=scale), [grad_shape], scalars=3)(*place, own)
    grad_one, grad_two = call(
        functools.partial(unpack_other_kernel, scale=scale),
        [grad_shape, grad_shape],
        [pltpu.VMEM(grad_shape.shape, F32), pltpu.SemaphoreType.DMA((2,))],
        scalars=3,
        inside=False,
    )(*place, mine, other)

    half_b = jax.ShapeDtypeStruct((tile_x, tile_y // 2, chans, tile_z), BF16)
    low, pre_pad = call(
        branch_low_kernel, [half_b, pad_b], scalars=3, flops=flops // 2
    )(*place, mask_f, w_branch, masked_grad, pre_grad, *pre_xr, *pre_yr)
    (high,) = call(branch_high_kernel, [half_b], flops=flops // 2)(mask_f, w_branch, masked_grad, pre_pad)
    grad_features = jnp.transpose(jnp.concatenate([low, high], axis=1), (2, 0, 1, 3))
    return grad_features, grad_one, grad_two


def solution(mesh):
    placed = (P(None, "gx", "gy", None), P(None, "gx", "gy", None), P("gx", "gy", None), P(), P())
    return jax.shard_map(
        body,
        mesh=mesh,
        in_specs=placed,
        out_specs=(P(None, "gx", "gy", None), P(), P()),
        check_vma=False,
    )
```

```python
import functools
import math

import jax
import jax.numpy as jnp
from jax import lax
from jax.experimental import pallas as pl
from jax.experimental.pallas import tpu as pltpu
from jax.sharding import PartitionSpec as P


F32 = jnp.float32
BF16 = jnp.bfloat16
AXES = ("gx", "gy")


def swap_perms(count):
    even = [(i, i ^ 1) for i in range(count)]
    odd = [(i, i + 1 if i % 2 else i - 1) for i in range(1, count - 1)]
    return even, odd


def xor_permute(value, mask):
    total = lax.axis_size("gx") * lax.axis_size("gy")
    return lax.ppermute(value, AXES, [(i, i ^ mask) for i in range(total)])


def swap(value_even, value_odd, axis):
    even, odd = swap_perms(lax.axis_size(axis))
    return lax.ppermute(value_even, axis, even), lax.ppermute(value_odd, axis, odd)


def stack_row(stack, at_x, first_y, row):
    count, chans, depth = row.shape
    lane = lax.broadcasted_iota(jnp.int32, row.shape, 2)
    zero = jnp.zeros_like(row)
    below = jnp.where(lane == 0, zero, pltpu.roll(row, 1, 2))
    above = jnp.where(lane == depth - 1, zero, pltpu.roll(row, depth - 1, 2))
    ys = pl.ds(first_y, count)
    stack[at_x, ys, 0:chans, :] = below
    stack[at_x, ys, chans : 2 * chans, :] = row
    stack[at_x, ys, 2 * chans : 3 * chans, :] = above


def sides(parity, size):
    even = (1 - parity) * (size + 1)
    return even, size + 1 - even


def pad_tile(padded, place, tile, xr_even, xr_odd, yr_even, yr_odd, which):
    size_x, size_y = tile.shape[0], tile.shape[1]
    x_even, x_odd = sides(place[0], size_x)
    y_even, y_odd = sides(place[1], size_y)
    padded[x_even, 1 : size_y + 1] = xr_even[which]
    padded[x_odd, 1 : size_y + 1] = xr_odd[which]
    for i in range(size_x + 2):
        padded[i, y_even] = yr_even[i]
        padded[i, y_odd] = yr_odd[i]

    def body(i, carry):
        padded[i + 1, 1 : size_y + 1] = tile[i]
        return carry

    lax.fori_loop(0, size_x, body, 0)


def ypack_kernel(place, *refs):
    count = (len(refs) - 2) // 3
    tiles, (xr_even, xr_odd), outs = refs[:count], refs[count : count + 2], refs[count + 2 :]
    size_x, size_y = tiles[0].shape[0], tiles[0].shape[1]
    x_even, x_odd = sides(place[0], size_x)
    edges = (1 - place[1]) * (size_y - 1), place[1] * (size_y - 1)
    for k, tile in enumerate(tiles):
        for out, edge in zip(outs[2 * k : 2 * k + 2], edges):
            out[x_even] = xr_even[k, edge]
            out[x_odd] = xr_odd[k, edge]
            for i in range(size_x):
                out[i + 1] = tile[i, edge]


def conv_padded(padded, weights, first, count, emit):
    wide, _, chans, depth = padded.shape

    def body(x, carry):
        lane = lax.broadcasted_iota(jnp.int32, (chans, depth), 1)
        for y in range(first, first + count, 2):
            halves = []
            for side in range(2):
                at = y + side
                rows = [padded[x + a, at : at + 3].reshape(3 * chans, depth) for a in range(3)]
                halves.append(jnp.concatenate(rows, axis=0))
            out = jnp.dot(weights[...], jnp.concatenate(halves, axis=1), preferred_element_type=F32)
            for side in range(2):
                part = out[:, side * depth : (side + 1) * depth]
                below = jnp.where(lane == 0, 0.0, pltpu.roll(part[0:chans], 1, 1))
                above = jnp.where(lane == depth - 1, 0.0, pltpu.roll(part[2 * chans :], depth - 1, 1))
                emit(x, y + side, below + part[chans : 2 * chans] + above)
        return carry

    lax.fori_loop(0, wide - 2, body, 0)


def weights_kernel(one, two, w_pre, w_act, w_branch):
    chans = one.shape[-1]
    for kz in range(3):
        rows = slice(kz * chans, (kz + 1) * chans)
        taps = jnp.concatenate([one[a, b, kz] for a in range(3) for b in range(3)], axis=0)
        w_pre[rows] = taps.T
        for source, dest in ((two, w_act), (one, w_branch)):
            dest[rows] = jnp.concatenate(
                [source[2 - a, 2 - b, 2 - kz] for a in range(3) for b in range(3)], axis=1
            )


def forward_kernel(place, mask, weights, tile, xr_even, xr_odd, yr_even, yr_odd, activ, slope, padded):
    pad_tile(padded, place, tile, xr_even, xr_odd, yr_even, yr_odd, 0)

    def emit(x, y, value):
        sig = jax.nn.sigmoid(value)
        activ[x, y] = (mask[...] * (value * sig)).astype(BF16)
        slope[x, y] = mask[...] * (sig * (1.0 + value * (1.0 - sig)))

    conv_padded(padded, weights, 0, tile.shape[1], emit)


def backward_kernel(
    place, weights, slope, tile, xr_even, xr_odd, yr_even, yr_odd, pre_grad, xs_even, xs_odd, padded
):
    pad_tile(padded, place, tile, xr_even, xr_odd, yr_even, yr_odd, 1)
    size_x = tile.shape[0]

    def emit(x, y, value):
        pre_grad[x, y] = (slope[x, y] * value).astype(BF16)

    conv_padded(padded, weights, 0, tile.shape[1], emit)
    xs_even[0] = pre_grad[(1 - place[0]) * (size_x - 1)]
    xs_odd[0] = pre_grad[place[0] * (size_x - 1)]


def branch_part(mask, weights, base, padded, result, first):
    def emit(x, y, value):
        result[x, y - first] = (base[x, y].astype(F32) + mask[...] * value).astype(BF16)

    conv_padded(padded, weights, first, result.shape[1], emit)


def branch_low_kernel(place, mask, weights, base, tile, xr_even, xr_odd, yr_even, yr_odd, result, padded):
    pad_tile(padded, place, tile, xr_even, xr_odd, yr_even, yr_odd, 0)
    branch_part(mask, weights, base, padded, result, 0)


def branch_high_kernel(mask, weights, base, padded, result):
    branch_part(mask, weights, base, padded, result, base.shape[1] // 2)


def grad_accumulate(padded, stack, acc):
    size_x, size_y, _, _ = stack.shape
    acc[...] = jnp.zeros_like(acc)

    def body(i, carry):
        right = jnp.concatenate([stack[i, y] for y in range(size_y)], axis=1)
        left = []
        for a in range(3):
            rows = [padded[i + a, y] for y in range(size_y + 2)]
            for b in range(3):
                left.append(jnp.concatenate(rows[b : b + size_y], axis=1))
        left = jnp.concatenate(left, axis=0)
        acc[...] += lax.dot_general(left, right, (((1,), (1,)), ((), ())), preferred_element_type=F32)
        return carry

    lax.fori_loop(0, size_x, body, 0)


def pack_grad(dest, acc, chans):
    rows = acc.shape[0]
    half = rows // 2
    dest[0:rows] = acc[:, 0 : 2 * chans]
    low = acc[0:half, 2 * chans : 3 * chans]
    high = acc[half:rows, 2 * chans : 3 * chans]
    dest[rows : rows + half] = jnp.concatenate([low, high], axis=1)


def stack_tile(stack, source):
    def body(i, carry):
        stack_row(stack, i, 0, source[i])
        return carry

    lax.fori_loop(0, source.shape[0], body, 0)


def grad_two_kernel(grad_pad, activ, packed, stack, acc):
    stack_tile(stack, activ)
    grad_accumulate(grad_pad, stack, acc)
    pack_grad(packed, acc, activ.shape[2])


def grad_one_kernel(place, in_pad, pre_grad, packed_two, keep, send, stack, acc):
    stack_tile(stack, pre_grad)
    grad_accumulate(in_pad, stack, acc)

    @pl.when(place[0] == 0)
    def _():
        pack_grad(keep, acc, pre_grad.shape[2])
        send[...] = packed_two[...]

    @pl.when(place[0] != 0)
    def _():
        pack_grad(send, acc, pre_grad.shape[2])
        keep[...] = packed_two[...]


def split_kernel(place, keep, recv, *outs):
    rows = outs[0].shape[0]
    for dist, out in enumerate(outs):
        start = pl.multiple_of((place[2] ^ dist) * rows, 8)
        out[...] = keep[pl.ds(start, rows)] + recv[pl.ds(start, rows)]


def join_kernel(place, *refs):
    out = refs[-1]
    rows = refs[0].shape[0]
    for dist, part in enumerate(refs[:-1]):
        start = pl.multiple_of((place[2] ^ dist) * rows, 8)
        out[pl.ds(start, rows)] = part[...]


def unpack(scale, source, dest, second):
    chans = dest.shape[-1]
    rows = 9 * chans
    half, step = rows // 2, chans // 2
    for a in range(3):
        for b in range(3):
            start = (3 * a + b) * chans
            both = source[start : start + chans, :] * scale
            pieces = []
            for first in (start, start + step):
                if first < half:
                    pieces.append(source[rows + first : rows + first + step, 0:chans])
                else:
                    pieces.append(source[rows + first - half : rows + first - half + step, chans : 2 * chans])
            tail = jnp.concatenate(pieces, axis=0) * scale
            if second:
                both = both.T
                dest[2 - a, 2 - b, 0] = both[0:chans]
                dest[2 - a, 2 - b, 1] = both[chans : 2 * chans]
                dest[2 - a, 2 - b, 2] = tail.T
            else:
                dest[a, b, 2] = both[:, 0:chans]
                dest[a, b, 1] = both[:, chans : 2 * chans]
                dest[a, b, 0] = tail


def unpack_own_kernel(place, own, dest, *, scale):
    @pl.when(place[0] == 0)
    def _():
        unpack(scale, own, dest, False)

    @pl.when(place[0] != 0)
    def _():
        unpack(scale, own, dest, True)


def unpack_other_kernel(place, mine, other, grad_one, grad_two, held, sems, *, scale):
    def finish(own_dest, other_dest, second):
        first = pltpu.make_async_copy(mine, own_dest, sems.at[0])
        first.start()
        unpack(scale, other, held, second)
        last = pltpu.make_async_copy(held, other_dest, sems.at[1])
        last.start()
        first.wait()
        last.wait()

    @pl.when(place[0] == 0)
    def _():
        finish(grad_one, grad_two, True)

    @pl.when(place[0] != 0)
    def _():
        finish(grad_two, grad_one, False)


def call(kernel, outs, scratch=(), scalars=0, flops=0, inside=True):
    def wrapped(*refs):
        if scalars:
            kernel([ref[0] for ref in refs[:scalars]], *refs[scalars:])
        else:
            kernel(*refs)

    def run(*operands):
        specs = [pl.BlockSpec(memory_space=pltpu.SMEM)] * scalars
        specs += [pl.BlockSpec(memory_space=pltpu.VMEM)] * (len(operands) - scalars)
        moved = sum(o.size * o.dtype.itemsize for o in operands)
        moved += sum(math.prod(o.shape) * o.dtype.itemsize for o in outs)
        return pl.pallas_call(
            wrapped,
            out_shape=tuple(outs),
            in_specs=specs,
            out_specs=tuple(pl.BlockSpec(memory_space=pltpu.VMEM if inside else pl.ANY) for _ in outs),
            scratch_shapes=list(scratch),
            cost_estimate=pl.CostEstimate(flops=flops, bytes_accessed=moved, transcendentals=0),
            compiler_params=pltpu.CompilerParams(vmem_limit_bytes=40 * 1024 * 1024),
        )(*operands)

    return run


def body(features, cotangent, block_mask, kernel_one, kernel_two):
    chans, tile_x, tile_y, tile_z = features.shape
    blocks = block_mask.shape[2]
    cells_all = tile_x * tile_y * tile_z * lax.axis_size("gx") * lax.axis_size("gy")
    scale = 1.0 / math.sqrt(cells_all)
    place_x, place_y = lax.axis_index("gx"), lax.axis_index("gy")
    x_odd, y_odd = place_x & 1, place_y & 1
    place = [v.astype(jnp.int32).reshape(1) for v in (x_odd, y_odd, (place_x >> 1) & 3)]

    mask = jnp.broadcast_to(block_mask.reshape(blocks, 1), (blocks, tile_z // blocks)).reshape(1, tile_z)
    mask_f = mask.astype(F32)
    mask_b = mask.astype(BF16).reshape(1, 1, tile_z)

    def x_edges(at):
        both = [lax.dynamic_index_in_dim(a, at, 1, keepdims=False) * mask_b for a in (features, cotangent)]
        return jnp.stack([jnp.transpose(a, (1, 0, 2)) for a in both])

    xr = swap(x_edges((1 - x_odd) * (tile_x - 1)), x_edges(x_odd * (tile_x - 1)), "gx")
    masked_in = jnp.transpose(features * mask_b[:, None], (1, 2, 0, 3))
    masked_grad = jnp.transpose(cotangent * mask_b[:, None], (1, 2, 0, 3))

    tile_shape = (tile_x, tile_y, chans, tile_z)
    tile_b = jax.ShapeDtypeStruct(tile_shape, BF16)
    column_b = jax.ShapeDtypeStruct((tile_x + 2, chans, tile_z), BF16)
    edge_b = jax.ShapeDtypeStruct((1, tile_y, chans, tile_z), BF16)
    pad_b = jax.ShapeDtypeStruct((tile_x + 2, tile_y + 2, chans, tile_z), BF16)
    flops = 2 * 27 * chans * chans * tile_x * tile_y * tile_z

    def y_sends(tiles, halo_x):
        outs = [column_b] * (2 * len(tiles))
        return call(ypack_kernel, outs, scalars=3)(*place, *tiles, *halo_x)

    sends = y_sends((masked_in, masked_grad), xr)
    matrix = jax.ShapeDtypeStruct((3 * chans, 9 * chans), BF16)
    even, odd = swap_perms(lax.axis_size("gy"))
    in_even = lax.ppermute(sends[0], "gy", even)
    w_pre, w_act, w_branch = call(weights_kernel, [matrix] * 3)(kernel_one, kernel_two)
    in_next, w_pre = lax.optimization_barrier((sends[1], w_pre))
    in_odd = lax.ppermute(in_next, "gy", odd)
    in_y = (in_even, in_odd)
    grad_y = swap(*sends[2:], "gy")

    tile_s = pltpu.VMEM((tile_x, tile_y, 3 * chans, tile_z), BF16)
    grad_s = pltpu.VMEM((9 * chans, 3 * chans), F32)

    activ, slope, in_pad = call(
        forward_kernel, [tile_b, jax.ShapeDtypeStruct(tile_shape, F32), pad_b], scalars=3, flops=flops
    )(*place, mask_f, w_pre, masked_in, *xr, *in_y)
    pre_grad, xs_even, xs_odd, grad_pad = call(
        backward_kernel, [tile_b, edge_b, edge_b, pad_b], scalars=3, flops=flops
    )(*place, w_act, slope, masked_grad, *xr, *grad_y)

    packed = 27 * chans * chans // (2 * chans)
    half = jax.ShapeDtypeStruct((packed, 2 * chans), F32)
    pre_xr = swap(xs_even, xs_odd, "gx")
    (packed_two,) = call(grad_two_kernel, [half], [tile_s, grad_s], flops=flops)(grad_pad, activ)
    pre_sends = y_sends((pre_grad,), pre_xr)
    pre_even = lax.ppermute(pre_sends[0], "gy", even)
    pre_odd = lax.ppermute(pre_sends[1], "gy", odd)
    pre_yr = (pre_even, pre_odd)
    keep, send = call(grad_one_kernel, [half, half], [tile_s, grad_s], scalars=3, flops=flops)(
        *place, in_pad, pre_grad, packed_two
    )

    recv = xor_permute(send, 8)
    chunk = jax.ShapeDtypeStruct((packed // 4, 2 * chans), F32)
    parts = call(split_kernel, [chunk] * 4, scalars=3)(*place, keep, recv)
    parts = [parts[0]] + [xor_permute(parts[d], 16 * d) for d in range(1, 4)]
    part = (parts[0] + parts[1]) + (parts[2] + parts[3])
    for masks in ((2, 4, 6), (1, 64, 65)):
        near, mid, far = [xor_permute(part, m) for m in masks]
        part = (part + near) + (mid + far)
    pieces = [part] + [xor_permute(part, 16 * d) for d in range(1, 4)]
    (own,) = call(join_kernel, [half], scalars=3)(*place, *pieces)
    other = xor_permute(own, 8)
    grad_shape = jax.ShapeDtypeStruct((3, 3, 3, chans, chans), F32)

    (mine,) = call(functools.partial(unpack_own_kernel, scale=scale), [grad_shape], scalars=3)(*place, own)
    grad_one, grad_two = call(
        functools.partial(unpack_other_kernel, scale=scale),
        [grad_shape, grad_shape],
        [pltpu.VMEM(grad_shape.shape, F32), pltpu.SemaphoreType.DMA((2,))],
        scalars=3,
        inside=False,
    )(*place, mine, other)

    half_b = jax.ShapeDtypeStruct((tile_x, tile_y // 2, chans, tile_z), BF16)
    low, pre_pad = call(
        branch_low_kernel, [half_b, pad_b], scalars=3, flops=flops // 2
    )(*place, mask_f, w_branch, masked_grad, pre_grad, *pre_xr, *pre_yr)
    (high,) = call(branch_high_kernel, [half_b], flops=flops // 2)(mask_f, w_branch, masked_grad, pre_pad)
    grad_features = jnp.transpose(jnp.concatenate([low, high], axis=1), (2, 0, 1, 3))
    return grad_features, grad_one, grad_two


def solution(mesh):
    placed = (P(None, "gx", "gy", None), P(None, "gx", "gy", None), P("gx", "gy", None), P(), P())
    return jax.shard_map(
        body,
        mesh=mesh,
        in_specs=placed,
        out_specs=(P(None, "gx", "gy", None), P(), P()),
        check_vma=False,
    )
```

```python
import functools
import math

import jax
import jax.numpy as jnp
from jax import lax
from jax.experimental import pallas as pl
from jax.experimental.pallas import tpu as pltpu
from jax.sharding import PartitionSpec as P


F32 = jnp.float32
BF16 = jnp.bfloat16
AXES = ("gx", "gy")


def swap_perms(count):
    even = [(i, i ^ 1) for i in range(count)]
    odd = [(i, i + 1 if i % 2 else i - 1) for i in range(1, count - 1)]
    return even, odd


def xor_permute(value, mask):
    total = lax.axis_size("gx") * lax.axis_size("gy")
    return lax.ppermute(value, AXES, [(i, i ^ mask) for i in range(total)])


def swap(value_even, value_odd, axis):
    even, odd = swap_perms(lax.axis_size(axis))
    return lax.ppermute(value_even, axis, even), lax.ppermute(value_odd, axis, odd)


def stack_row(stack, at_x, first_y, row):
    count, chans, depth = row.shape
    lane = lax.broadcasted_iota(jnp.int32, row.shape, 2)
    zero = jnp.zeros_like(row)
    below = jnp.where(lane == 0, zero, pltpu.roll(row, 1, 2))
    above = jnp.where(lane == depth - 1, zero, pltpu.roll(row, depth - 1, 2))
    ys = pl.ds(first_y, count)
    stack[at_x, ys, 0:chans, :] = below
    stack[at_x, ys, chans : 2 * chans, :] = row
    stack[at_x, ys, 2 * chans : 3 * chans, :] = above


def store_shifted(stack, x, y, value):
    chans, depth = value.shape
    lane = lax.broadcasted_iota(jnp.int32, value.shape, 1)
    below = jnp.where(lane == 0, 0.0, pltpu.roll(value, 1, 1))
    above = jnp.where(lane == depth - 1, 0.0, pltpu.roll(value, depth - 1, 1))
    stack[x, y, 0:chans] = below.astype(BF16)
    stack[x, y, chans : 2 * chans] = value.astype(BF16)
    stack[x, y, 2 * chans : 3 * chans] = above.astype(BF16)


def sides(parity, size):
    even = (1 - parity) * (size + 1)
    return even, size + 1 - even


def pad_tile(padded, place, tile, xr_even, xr_odd, yr_even, yr_odd, which):
    size_x, size_y = tile.shape[0], tile.shape[1]
    x_even, x_odd = sides(place[0], size_x)
    y_even, y_odd = sides(place[1], size_y)
    padded[x_even, 1 : size_y + 1] = xr_even[which]
    padded[x_odd, 1 : size_y + 1] = xr_odd[which]
    for i in range(size_x + 2):
        padded[i, y_even] = yr_even[i]
        padded[i, y_odd] = yr_odd[i]

    def body(i, carry):
        padded[i + 1, 1 : size_y + 1] = tile[i]
        return carry

    lax.fori_loop(0, size_x, body, 0)


def ypack_kernel(place, *refs):
    count = (len(refs) - 2) // 3
    tiles, (xr_even, xr_odd), outs = refs[:count], refs[count : count + 2], refs[count + 2 :]
    size_x, size_y = tiles[0].shape[0], tiles[0].shape[1]
    x_even, x_odd = sides(place[0], size_x)
    edges = (1 - place[1]) * (size_y - 1), place[1] * (size_y - 1)
    for k, tile in enumerate(tiles):
        for out, edge in zip(outs[2 * k : 2 * k + 2], edges):
            out[x_even] = xr_even[k, edge]
            out[x_odd] = xr_odd[k, edge]
            for i in range(size_x):
                out[i + 1] = tile[i, edge]


def conv_padded(padded, weights, first, count, emit):
    wide, _, chans, depth = padded.shape

    def body(x, carry):
        lane = lax.broadcasted_iota(jnp.int32, (chans, depth), 1)
        for y in range(first, first + count, 2):
            halves = []
            for side in range(2):
                at = y + side
                rows = [padded[x + a, at : at + 3].reshape(3 * chans, depth) for a in range(3)]
                halves.append(jnp.concatenate(rows, axis=0))
            out = jnp.dot(weights[...], jnp.concatenate(halves, axis=1), preferred_element_type=F32)
            for side in range(2):
                part = out[:, side * depth : (side + 1) * depth]
                below = jnp.where(lane == 0, 0.0, pltpu.roll(part[0:chans], 1, 1))
                above = jnp.where(lane == depth - 1, 0.0, pltpu.roll(part[2 * chans :], depth - 1, 1))
                emit(x, y + side, below + part[chans : 2 * chans] + above)
        return carry

    lax.fori_loop(0, wide - 2, body, 0)


def weights_kernel(one, two, w_pre, w_act, w_branch):
    chans = one.shape[-1]
    for kz in range(3):
        rows = slice(kz * chans, (kz + 1) * chans)
        taps = jnp.concatenate([one[a, b, kz] for a in range(3) for b in range(3)], axis=0)
        w_pre[rows] = taps.T
        for source, dest in ((two, w_act), (one, w_branch)):
            dest[rows] = jnp.concatenate(
                [source[2 - a, 2 - b, 2 - kz] for a in range(3) for b in range(3)], axis=1
            )


def forward_kernel(place, mask, weights, tile, xr_even, xr_odd, yr_even, yr_odd, activ, slope, padded):
    pad_tile(padded, place, tile, xr_even, xr_odd, yr_even, yr_odd, 0)

    def emit(x, y, value):
        sig = jax.nn.sigmoid(value)
        store_shifted(activ, x, y, mask[...] * (value * sig))
        slope[x, y] = mask[...] * (sig * (1.0 + value * (1.0 - sig)))

    conv_padded(padded, weights, 0, tile.shape[1], emit)


def backward_kernel(
    place, weights, slope, tile, xr_even, xr_odd, yr_even, yr_odd, pre_grad, xs_even, xs_odd, padded
):
    pad_tile(padded, place, tile, xr_even, xr_odd, yr_even, yr_odd, 1)
    size_x = tile.shape[0]

    def emit(x, y, value):
        pre_grad[x, y] = (slope[x, y] * value).astype(BF16)

    conv_padded(padded, weights, 0, tile.shape[1], emit)
    xs_even[0] = pre_grad[(1 - place[0]) * (size_x - 1)]
    xs_odd[0] = pre_grad[place[0] * (size_x - 1)]


def branch_part(mask, weights, base, padded, result, first):
    def emit(x, y, value):
        result[x, y - first] = (base[x, y].astype(F32) + mask[...] * value).astype(BF16)

    conv_padded(padded, weights, first, result.shape[1], emit)


def branch_first_kernel(place, mask, weights, base, tile, xr_even, xr_odd, yr_even, yr_odd, result, padded):
    pad_tile(padded, place, tile, xr_even, xr_odd, yr_even, yr_odd, 0)
    branch_part(mask, weights, base, padded, result, 0)


def branch_next_kernel(mask, weights, base, padded, result, *, first):
    branch_part(mask, weights, base, padded, result, first)


def grad_accumulate(padded, stack, acc):
    size_x, size_y, _, _ = stack.shape
    acc[...] = jnp.zeros_like(acc)

    def body(i, carry):
        right = jnp.concatenate([stack[i, y] for y in range(size_y)], axis=1)
        left = []
        for a in range(3):
            rows = [padded[i + a, y] for y in range(size_y + 2)]
            for b in range(3):
                left.append(jnp.concatenate(rows[b : b + size_y], axis=1))
        left = jnp.concatenate(left, axis=0)
        acc[...] += lax.dot_general(left, right, (((1,), (1,)), ((), ())), preferred_element_type=F32)
        return carry

    lax.fori_loop(0, size_x, body, 0)


def pack_grad(dest, acc, chans):
    rows = acc.shape[0]
    half = rows // 2
    dest[0:rows] = acc[:, 0 : 2 * chans]
    low = acc[0:half, 2 * chans : 3 * chans]
    high = acc[half:rows, 2 * chans : 3 * chans]
    dest[rows : rows + half] = jnp.concatenate([low, high], axis=1)


def stack_tile(stack, source):
    def body(i, carry):
        stack_row(stack, i, 0, source[i])
        return carry

    lax.fori_loop(0, source.shape[0], body, 0)


def grad_two_kernel(grad_pad, activ, packed, acc):
    grad_accumulate(grad_pad, activ, acc)
    pack_grad(packed, acc, grad_pad.shape[2])


def grad_one_kernel(place, in_pad, pre_grad, packed_two, keep, send, stack, acc):
    stack_tile(stack, pre_grad)
    grad_accumulate(in_pad, stack, acc)

    @pl.when(place[0] == 0)
    def _():
        pack_grad(keep, acc, pre_grad.shape[2])
        send[...] = packed_two[...]

    @pl.when(place[0] != 0)
    def _():
        pack_grad(send, acc, pre_grad.shape[2])
        keep[...] = packed_two[...]


def split_kernel(place, keep, recv, *outs):
    rows = outs[0].shape[0]
    for dist, out in enumerate(outs):
        start = pl.multiple_of((place[2] ^ dist) * rows, 8)
        out[...] = keep[pl.ds(start, rows)] + recv[pl.ds(start, rows)]


def join_kernel(place, *refs):
    out = refs[-1]
    rows = refs[0].shape[0]
    for dist, part in enumerate(refs[:-1]):
        start = pl.multiple_of((place[2] ^ dist) * rows, 8)
        out[pl.ds(start, rows)] = part[...]


def unpack(scale, source, dest, second):
    chans = dest.shape[-1]
    rows = 9 * chans
    half, step = rows // 2, chans // 2
    for a in range(3):
        for b in range(3):
            start = (3 * a + b) * chans
            both = source[start : start + chans, :] * scale
            pieces = []
            for first in (start, start + step):
                if first < half:
                    pieces.append(source[rows + first : rows + first + step, 0:chans])
                else:
                    pieces.append(source[rows + first - half : rows + first - half + step, chans : 2 * chans])
            tail = jnp.concatenate(pieces, axis=0) * scale
            if second:
                both = both.T
                dest[2 - a, 2 - b, 0] = both[0:chans]
                dest[2 - a, 2 - b, 1] = both[chans : 2 * chans]
                dest[2 - a, 2 - b, 2] = tail.T
            else:
                dest[a, b, 2] = both[:, 0:chans]
                dest[a, b, 1] = both[:, chans : 2 * chans]
                dest[a, b, 0] = tail


def unpack_own_kernel(place, own, dest, *, scale):
    @pl.when(place[0] == 0)
    def _():
        unpack(scale, own, dest, False)

    @pl.when(place[0] != 0)
    def _():
        unpack(scale, own, dest, True)


def unpack_other_kernel(place, mine, other, grad_one, grad_two, held, sems, *, scale):
    def finish(own_dest, other_dest, second):
        first = pltpu.make_async_copy(mine, own_dest, sems.at[0])
        first.start()
        unpack(scale, other, held, second)
        last = pltpu.make_async_copy(held, other_dest, sems.at[1])
        last.start()
        first.wait()
        last.wait()

    @pl.when(place[0] == 0)
    def _():
        finish(grad_one, grad_two, True)

    @pl.when(place[0] != 0)
    def _():
        finish(grad_two, grad_one, False)


def call(kernel, outs, scratch=(), scalars=0, flops=0, inside=True):
    def wrapped(*refs):
        if scalars:
            kernel([ref[0] for ref in refs[:scalars]], *refs[scalars:])
        else:
            kernel(*refs)

    def run(*operands):
        specs = [pl.BlockSpec(memory_space=pltpu.SMEM)] * scalars
        specs += [pl.BlockSpec(memory_space=pltpu.VMEM)] * (len(operands) - scalars)
        moved = sum(o.size * o.dtype.itemsize for o in operands)
        moved += sum(math.prod(o.shape) * o.dtype.itemsize for o in outs)
        return pl.pallas_call(
            wrapped,
            out_shape=tuple(outs),
            in_specs=specs,
            out_specs=tuple(pl.BlockSpec(memory_space=pltpu.VMEM if inside else pl.ANY) for _ in outs),
            scratch_shapes=list(scratch),
            cost_estimate=pl.CostEstimate(flops=flops, bytes_accessed=moved, transcendentals=0),
            compiler_params=pltpu.CompilerParams(vmem_limit_bytes=40 * 1024 * 1024),
        )(*operands)

    return run


def body(features, cotangent, block_mask, kernel_one, kernel_two):
    chans, tile_x, tile_y, tile_z = features.shape
    blocks = block_mask.shape[2]
    cells_all = tile_x * tile_y * tile_z * lax.axis_size("gx") * lax.axis_size("gy")
    scale = 1.0 / math.sqrt(cells_all)
    place_x, place_y = lax.axis_index("gx"), lax.axis_index("gy")
    x_odd, y_odd = place_x & 1, place_y & 1
    place = [v.astype(jnp.int32).reshape(1) for v in (x_odd, y_odd, (place_x >> 1) & 3)]

    mask = jnp.broadcast_to(block_mask.reshape(blocks, 1), (blocks, tile_z // blocks)).reshape(1, tile_z)
    mask_f = mask.astype(F32)
    mask_b = mask.astype(BF16).reshape(1, 1, tile_z)

    def x_edges(at):
        both = [lax.dynamic_index_in_dim(a, at, 1, keepdims=False) * mask_b for a in (features, cotangent)]
        return jnp.stack([jnp.transpose(a, (1, 0, 2)) for a in both])

    xr = swap(x_edges((1 - x_odd) * (tile_x - 1)), x_edges(x_odd * (tile_x - 1)), "gx")
    masked_in = jnp.transpose(features * mask_b[:, None], (1, 2, 0, 3))
    masked_grad = jnp.transpose(cotangent * mask_b[:, None], (1, 2, 0, 3))

    tile_shape = (tile_x, tile_y, chans, tile_z)
    tile_b = jax.ShapeDtypeStruct(tile_shape, BF16)
    column_b = jax.ShapeDtypeStruct((tile_x + 2, chans, tile_z), BF16)
    edge_b = jax.ShapeDtypeStruct((1, tile_y, chans, tile_z), BF16)
    pad_b = jax.ShapeDtypeStruct((tile_x + 2, tile_y + 2, chans, tile_z), BF16)
    flops = 2 * 27 * chans * chans * tile_x * tile_y * tile_z

    def y_sends(tiles, halo_x):
        outs = [column_b] * (2 * len(tiles))
        return call(ypack_kernel, outs, scalars=3)(*place, *tiles, *halo_x)

    sends = y_sends((masked_in, masked_grad), xr)
    matrix = jax.ShapeDtypeStruct((3 * chans, 9 * chans), BF16)
    even, odd = swap_perms(lax.axis_size("gy"))
    in_even = lax.ppermute(sends[0], "gy", even)
    w_pre, w_act, w_branch = call(weights_kernel, [matrix] * 3)(kernel_one, kernel_two)
    in_next, w_pre = lax.optimization_barrier((sends[1], w_pre))
    in_odd = lax.ppermute(in_next, "gy", odd)
    in_y = (in_even, in_odd)
    grad_y = swap(*sends[2:], "gy")

    tile_s = pltpu.VMEM((tile_x, tile_y, 3 * chans, tile_z), BF16)
    shifted_b = jax.ShapeDtypeStruct((tile_x, tile_y, 3 * chans, tile_z), BF16)
    grad_s = pltpu.VMEM((9 * chans, 3 * chans), F32)

    activ, slope, in_pad = call(
        forward_kernel, [shifted_b, jax.ShapeDtypeStruct(tile_shape, F32), pad_b], scalars=3, flops=flops
    )(*place, mask_f, w_pre, masked_in, *xr, *in_y)
    pre_grad, xs_even, xs_odd, grad_pad = call(
        backward_kernel, [tile_b, edge_b, edge_b, pad_b], scalars=3, flops=flops
    )(*place, w_act, slope, masked_grad, *xr, *grad_y)

    packed = 27 * chans * chans // (2 * chans)
    half = jax.ShapeDtypeStruct((packed, 2 * chans), F32)
    pre_xr = swap(xs_even, xs_odd, "gx")
    (packed_two,) = call(grad_two_kernel, [half], [grad_s], flops=flops)(grad_pad, activ)
    pre_sends = y_sends((pre_grad,), pre_xr)
    pre_even = lax.ppermute(pre_sends[0], "gy", even)
    pre_odd = lax.ppermute(pre_sends[1], "gy", odd)
    pre_yr = (pre_even, pre_odd)
    keep, send = call(grad_one_kernel, [half, half], [tile_s, grad_s], scalars=3, flops=flops)(
        *place, in_pad, pre_grad, packed_two
    )

    recv = xor_permute(send, 8)
    chunk = jax.ShapeDtypeStruct((packed // 4, 2 * chans), F32)
    parts = call(split_kernel, [chunk] * 4, scalars=3)(*place, keep, recv)
    parts = [parts[0]] + [xor_permute(parts[d], 16 * d) for d in range(1, 4)]
    part = (parts[0] + parts[1]) + (parts[2] + parts[3])
    for masks in ((2, 4, 6), (1, 64, 65)):
        near, mid, far = [xor_permute(part, m) for m in masks]
        part = (part + near) + (mid + far)
    pieces = [part] + [xor_permute(part, 16 * d) for d in range(1, 4)]
    (own,) = call(join_kernel, [half], scalars=3)(*place, *pieces)
    other = xor_permute(own, 8)
    grad_shape = jax.ShapeDtypeStruct((3, 3, 3, chans, chans), F32)

    (mine,) = call(functools.partial(unpack_own_kernel, scale=scale), [grad_shape], scalars=3)(*place, own)
    grad_one, grad_two = call(
        functools.partial(unpack_other_kernel, scale=scale),
        [grad_shape, grad_shape],
        [pltpu.VMEM(grad_shape.shape, F32), pltpu.SemaphoreType.DMA((2,))],
        scalars=3,
        inside=False,
    )(*place, mine, other)

    cuts = (0, tile_y // 4, tile_y // 2, tile_y)

    def rows_b(k):
        return [jax.ShapeDtypeStruct((tile_x, cuts[k + 1] - cuts[k], chans, tile_z), BF16)]

    piece, pre_pad = call(
        branch_first_kernel, rows_b(0) + [pad_b], scalars=3, flops=flops // 4
    )(*place, mask_f, w_branch, masked_grad, pre_grad, *pre_xr, *pre_yr)
    pieces = [piece]
    for k in (1, 2):
        kernel = functools.partial(branch_next_kernel, first=cuts[k])
        pieces += call(kernel, rows_b(k), flops=flops // 4 * k)(mask_f, w_branch, masked_grad, pre_pad)
    grad_features = jnp.transpose(jnp.concatenate(pieces, axis=1), (2, 0, 1, 3))
    return grad_features, grad_one, grad_two


def solution(mesh):
    placed = (P(None, "gx", "gy", None), P(None, "gx", "gy", None), P("gx", "gy", None), P(), P())
    return jax.shard_map(
        body,
        mesh=mesh,
        in_specs=placed,
        out_specs=(P(None, "gx", "gy", None), P(), P()),
        check_vma=False,
    )
```

```python
import functools
import math

import jax
import jax.numpy as jnp
from jax import lax
from jax.experimental import pallas as pl
from jax.experimental.pallas import tpu as pltpu
from jax.sharding import PartitionSpec as P


F32 = jnp.float32
BF16 = jnp.bfloat16
AXES = ("gx", "gy")


def swap_perms(count):
    even = [(i, i ^ 1) for i in range(count)]
    odd = [(i, i + 1 if i % 2 else i - 1) for i in range(1, count - 1)]
    return even, odd


def xor_permute(value, mask):
    total = lax.axis_size("gx") * lax.axis_size("gy")
    return lax.ppermute(value, AXES, [(i, i ^ mask) for i in range(total)])


def swap(value_even, value_odd, axis):
    even, odd = swap_perms(lax.axis_size(axis))
    return lax.ppermute(value_even, axis, even), lax.ppermute(value_odd, axis, odd)


def stack_row(stack, at_x, first_y, row):
    count, chans, depth = row.shape
    lane = lax.broadcasted_iota(jnp.int32, row.shape, 2)
    zero = jnp.zeros_like(row)
    below = jnp.where(lane == 0, zero, pltpu.roll(row, 1, 2))
    above = jnp.where(lane == depth - 1, zero, pltpu.roll(row, depth - 1, 2))
    ys = pl.ds(first_y, count)
    stack[at_x, ys, 0:chans, :] = below
    stack[at_x, ys, chans : 2 * chans, :] = row
    stack[at_x, ys, 2 * chans : 3 * chans, :] = above


def store_shifted(stack, x, y, value):
    chans, depth = value.shape
    lane = lax.broadcasted_iota(jnp.int32, value.shape, 1)
    below = jnp.where(lane == 0, 0.0, pltpu.roll(value, 1, 1))
    above = jnp.where(lane == depth - 1, 0.0, pltpu.roll(value, depth - 1, 1))
    stack[x, y, 0:chans] = below.astype(BF16)
    stack[x, y, chans : 2 * chans] = value.astype(BF16)
    stack[x, y, 2 * chans : 3 * chans] = above.astype(BF16)


def sides(parity, size):
    even = (1 - parity) * (size + 1)
    return even, size + 1 - even


def pad_tile(padded, place, tile, xr_even, xr_odd, yr_even, yr_odd, which):
    size_x, size_y = tile.shape[0], tile.shape[1]
    x_even, x_odd = sides(place[0], size_x)
    y_even, y_odd = sides(place[1], size_y)
    padded[x_even, 1 : size_y + 1] = xr_even[which]
    padded[x_odd, 1 : size_y + 1] = xr_odd[which]
    for i in range(size_x + 2):
        padded[i, y_even] = yr_even[i]
        padded[i, y_odd] = yr_odd[i]

    def body(i, carry):
        padded[i + 1, 1 : size_y + 1] = tile[i]
        return carry

    lax.fori_loop(0, size_x, body, 0)


def ypack_kernel(place, *refs):
    count = (len(refs) - 2) // 3
    tiles, (xr_even, xr_odd), outs = refs[:count], refs[count : count + 2], refs[count + 2 :]
    size_x, size_y = tiles[0].shape[0], tiles[0].shape[1]
    x_even, x_odd = sides(place[0], size_x)
    edges = (1 - place[1]) * (size_y - 1), place[1] * (size_y - 1)
    for k, tile in enumerate(tiles):
        for out, edge in zip(outs[2 * k : 2 * k + 2], edges):
            out[x_even] = xr_even[k, edge]
            out[x_odd] = xr_odd[k, edge]
            for i in range(size_x):
                out[i + 1] = tile[i, edge]


def conv_padded(padded, weights, first, count, emit):
    wide, _, chans, depth = padded.shape

    def body(x, carry):
        lane = lax.broadcasted_iota(jnp.int32, (chans, depth), 1)
        for y in range(first, first + count, 2):
            halves = []
            for side in range(2):
                at = y + side
                rows = [padded[x + a, at : at + 3].reshape(3 * chans, depth) for a in range(3)]
                halves.append(jnp.concatenate(rows, axis=0))
            out = jnp.dot(weights[...], jnp.concatenate(halves, axis=1), preferred_element_type=F32)
            for side in range(2):
                part = out[:, side * depth : (side + 1) * depth]
                below = jnp.where(lane == 0, 0.0, pltpu.roll(part[0:chans], 1, 1))
                above = jnp.where(lane == depth - 1, 0.0, pltpu.roll(part[2 * chans :], depth - 1, 1))
                emit(x, y + side, below + part[chans : 2 * chans] + above)
        return carry

    lax.fori_loop(0, wide - 2, body, 0, unroll=4)


def weights_kernel(one, two, w_pre, w_act, w_branch):
    chans = one.shape[-1]
    for kz in range(3):
        rows = slice(kz * chans, (kz + 1) * chans)
        taps = jnp.concatenate([one[a, b, kz] for a in range(3) for b in range(3)], axis=0)
        w_pre[rows] = taps.T
        for source, dest in ((two, w_act), (one, w_branch)):
            dest[rows] = jnp.concatenate(
                [source[2 - a, 2 - b, 2 - kz] for a in range(3) for b in range(3)], axis=1
            )


def forward_kernel(place, mask, weights, tile, xr_even, xr_odd, yr_even, yr_odd, activ, slope, padded):
    pad_tile(padded, place, tile, xr_even, xr_odd, yr_even, yr_odd, 0)

    def emit(x, y, value):
        sig = jax.nn.sigmoid(value)
        store_shifted(activ, x, y, mask[...] * (value * sig))
        slope[x, y] = mask[...] * (sig * (1.0 + value * (1.0 - sig)))

    conv_padded(padded, weights, 0, tile.shape[1], emit)


def backward_kernel(
    place, weights, slope, tile, xr_even, xr_odd, yr_even, yr_odd, pre_grad, xs_even, xs_odd, padded
):
    pad_tile(padded, place, tile, xr_even, xr_odd, yr_even, yr_odd, 1)
    size_x = tile.shape[0]

    def emit(x, y, value):
        pre_grad[x, y] = (slope[x, y] * value).astype(BF16)

    conv_padded(padded, weights, 0, tile.shape[1], emit)
    xs_even[0] = pre_grad[(1 - place[0]) * (size_x - 1)]
    xs_odd[0] = pre_grad[place[0] * (size_x - 1)]


def branch_part(mask, weights, base, padded, result, first):
    def emit(x, y, value):
        result[x, y - first] = (base[x, y].astype(F32) + mask[...] * value).astype(BF16)

    conv_padded(padded, weights, first, result.shape[1], emit)


def branch_first_kernel(place, mask, weights, base, tile, xr_even, xr_odd, yr_even, yr_odd, result, padded):
    pad_tile(padded, place, tile, xr_even, xr_odd, yr_even, yr_odd, 0)
    branch_part(mask, weights, base, padded, result, 0)


def branch_next_kernel(mask, weights, base, padded, result, *, first):
    branch_part(mask, weights, base, padded, result, first)


def grad_accumulate(padded, stack, acc):
    size_x, size_y, _, _ = stack.shape
    acc[...] = jnp.zeros_like(acc)

    def body(i, carry):
        right = jnp.concatenate([stack[i, y] for y in range(size_y)], axis=1)
        left = []
        for a in range(3):
            rows = [padded[i + a, y] for y in range(size_y + 2)]
            for b in range(3):
                left.append(jnp.concatenate(rows[b : b + size_y], axis=1))
        left = jnp.concatenate(left, axis=0)
        acc[...] += lax.dot_general(left, right, (((1,), (1,)), ((), ())), preferred_element_type=F32)
        return carry

    lax.fori_loop(0, size_x, body, 0, unroll=4)


def pack_grad(dest, acc, chans):
    rows = acc.shape[0]
    half = rows // 2
    dest[0:rows] = acc[:, 0 : 2 * chans]
    low = acc[0:half, 2 * chans : 3 * chans]
    high = acc[half:rows, 2 * chans : 3 * chans]
    dest[rows : rows + half] = jnp.concatenate([low, high], axis=1)


def stack_tile(stack, source):
    def body(i, carry):
        stack_row(stack, i, 0, source[i])
        return carry

    lax.fori_loop(0, source.shape[0], body, 0, unroll=4)


def grad_two_kernel(grad_pad, activ, packed, acc):
    grad_accumulate(grad_pad, activ, acc)
    pack_grad(packed, acc, grad_pad.shape[2])


def grad_one_kernel(place, in_pad, pre_grad, packed_two, keep, send, stack, acc):
    stack_tile(stack, pre_grad)
    grad_accumulate(in_pad, stack, acc)

    @pl.when(place[0] == 0)
    def _():
        pack_grad(keep, acc, pre_grad.shape[2])
        send[...] = packed_two[...]

    @pl.when(place[0] != 0)
    def _():
        pack_grad(send, acc, pre_grad.shape[2])
        keep[...] = packed_two[...]


def split_kernel(place, keep, recv, *outs):
    rows = outs[0].shape[0]
    for dist, out in enumerate(outs):
        start = pl.multiple_of((place[2] ^ dist) * rows, 8)
        out[...] = keep[pl.ds(start, rows)] + recv[pl.ds(start, rows)]


def join_kernel(place, *refs):
    out = refs[-1]
    rows = refs[0].shape[0]
    for dist, part in enumerate(refs[:-1]):
        start = pl.multiple_of((place[2] ^ dist) * rows, 8)
        out[pl.ds(start, rows)] = part[...]


def unpack(scale, source, dest, second):
    chans = dest.shape[-1]
    rows = 9 * chans
    half, step = rows // 2, chans // 2
    for a in range(3):
        for b in range(3):
            start = (3 * a + b) * chans
            both = source[start : start + chans, :] * scale
            pieces = []
            for first in (start, start + step):
                if first < half:
                    pieces.append(source[rows + first : rows + first + step, 0:chans])
                else:
                    pieces.append(source[rows + first - half : rows + first - half + step, chans : 2 * chans])
            tail = jnp.concatenate(pieces, axis=0) * scale
            if second:
                both = both.T
                dest[2 - a, 2 - b, 0] = both[0:chans]
                dest[2 - a, 2 - b, 1] = both[chans : 2 * chans]
                dest[2 - a, 2 - b, 2] = tail.T
            else:
                dest[a, b, 2] = both[:, 0:chans]
                dest[a, b, 1] = both[:, chans : 2 * chans]
                dest[a, b, 0] = tail


def unpack_own_kernel(place, own, dest, *, scale):
    @pl.when(place[0] == 0)
    def _():
        unpack(scale, own, dest, False)

    @pl.when(place[0] != 0)
    def _():
        unpack(scale, own, dest, True)


def unpack_other_kernel(place, mine, other, grad_one, grad_two, held, sems, *, scale):
    def finish(own_dest, other_dest, second):
        first = pltpu.make_async_copy(mine, own_dest, sems.at[0])
        first.start()
        unpack(scale, other, held, second)
        last = pltpu.make_async_copy(held, other_dest, sems.at[1])
        last.start()
        first.wait()
        last.wait()

    @pl.when(place[0] == 0)
    def _():
        finish(grad_one, grad_two, True)

    @pl.when(place[0] != 0)
    def _():
        finish(grad_two, grad_one, False)


def call(kernel, outs, scratch=(), scalars=0, flops=0, inside=True):
    def wrapped(*refs):
        if scalars:
            kernel([ref[0] for ref in refs[:scalars]], *refs[scalars:])
        else:
            kernel(*refs)

    def run(*operands):
        specs = [pl.BlockSpec(memory_space=pltpu.SMEM)] * scalars
        specs += [pl.BlockSpec(memory_space=pltpu.VMEM)] * (len(operands) - scalars)
        moved = sum(o.size * o.dtype.itemsize for o in operands)
        moved += sum(math.prod(o.shape) * o.dtype.itemsize for o in outs)
        return pl.pallas_call(
            wrapped,
            out_shape=tuple(outs),
            in_specs=specs,
            out_specs=tuple(pl.BlockSpec(memory_space=pltpu.VMEM if inside else pl.ANY) for _ in outs),
            scratch_shapes=list(scratch),
            cost_estimate=pl.CostEstimate(flops=flops, bytes_accessed=moved, transcendentals=0),
            compiler_params=pltpu.CompilerParams(vmem_limit_bytes=40 * 1024 * 1024),
        )(*operands)

    return run


def body(features, cotangent, block_mask, kernel_one, kernel_two):
    chans, tile_x, tile_y, tile_z = features.shape
    blocks = block_mask.shape[2]
    cells_all = tile_x * tile_y * tile_z * lax.axis_size("gx") * lax.axis_size("gy")
    scale = 1.0 / math.sqrt(cells_all)
    place_x, place_y = lax.axis_index("gx"), lax.axis_index("gy")
    x_odd, y_odd = place_x & 1, place_y & 1
    place = [v.astype(jnp.int32).reshape(1) for v in (x_odd, y_odd, (place_x >> 1) & 3)]

    mask = jnp.broadcast_to(block_mask.reshape(blocks, 1), (blocks, tile_z // blocks)).reshape(1, tile_z)
    mask_f = mask.astype(F32)
    mask_b = mask.astype(BF16).reshape(1, 1, tile_z)

    def x_edges(at):
        both = [lax.dynamic_index_in_dim(a, at, 1, keepdims=False) * mask_b for a in (features, cotangent)]
        return jnp.stack([jnp.transpose(a, (1, 0, 2)) for a in both])

    xr = swap(x_edges((1 - x_odd) * (tile_x - 1)), x_edges(x_odd * (tile_x - 1)), "gx")
    masked_in = jnp.transpose(features * mask_b[:, None], (1, 2, 0, 3))
    masked_grad = jnp.transpose(cotangent * mask_b[:, None], (1, 2, 0, 3))

    tile_shape = (tile_x, tile_y, chans, tile_z)
    tile_b = jax.ShapeDtypeStruct(tile_shape, BF16)
    column_b = jax.ShapeDtypeStruct((tile_x + 2, chans, tile_z), BF16)
    edge_b = jax.ShapeDtypeStruct((1, tile_y, chans, tile_z), BF16)
    pad_b = jax.ShapeDtypeStruct((tile_x + 2, tile_y + 2, chans, tile_z), BF16)
    flops = 2 * 27 * chans * chans * tile_x * tile_y * tile_z

    def y_sends(tiles, halo_x):
        outs = [column_b] * (2 * len(tiles))
        return call(ypack_kernel, outs, scalars=3)(*place, *tiles, *halo_x)

    sends = y_sends((masked_in, masked_grad), xr)
    matrix = jax.ShapeDtypeStruct((3 * chans, 9 * chans), BF16)
    even, odd = swap_perms(lax.axis_size("gy"))
    in_even = lax.ppermute(sends[0], "gy", even)
    w_pre, w_act, w_branch = call(weights_kernel, [matrix] * 3)(kernel_one, kernel_two)
    in_next, w_pre = lax.optimization_barrier((sends[1], w_pre))
    in_odd = lax.ppermute(in_next, "gy", odd)
    in_y = (in_even, in_odd)
    grad_y = swap(*sends[2:], "gy")

    tile_s = pltpu.VMEM((tile_x, tile_y, 3 * chans, tile_z), BF16)
    shifted_b = jax.ShapeDtypeStruct((tile_x, tile_y, 3 * chans, tile_z), BF16)
    grad_s = pltpu.VMEM((9 * chans, 3 * chans), F32)

    activ, slope, in_pad = call(
        forward_kernel, [shifted_b, jax.ShapeDtypeStruct(tile_shape, F32), pad_b], scalars=3, flops=flops
    )(*place, mask_f, w_pre, masked_in, *xr, *in_y)
    pre_grad, xs_even, xs_odd, grad_pad = call(
        backward_kernel, [tile_b, edge_b, edge_b, pad_b], scalars=3, flops=flops
    )(*place, w_act, slope, masked_grad, *xr, *grad_y)

    packed = 27 * chans * chans // (2 * chans)
    half = jax.ShapeDtypeStruct((packed, 2 * chans), F32)
    pre_xr = swap(xs_even, xs_odd, "gx")
    (packed_two,) = call(grad_two_kernel, [half], [grad_s], flops=flops)(grad_pad, activ)
    pre_sends = y_sends((pre_grad,), pre_xr)
    pre_even = lax.ppermute(pre_sends[0], "gy", even)
    pre_odd = lax.ppermute(pre_sends[1], "gy", odd)
    pre_yr = (pre_even, pre_odd)
    keep, send = call(grad_one_kernel, [half, half], [tile_s, grad_s], scalars=3, flops=flops)(
        *place, in_pad, pre_grad, packed_two
    )

    recv = xor_permute(send, 8)
    chunk = jax.ShapeDtypeStruct((packed // 4, 2 * chans), F32)
    parts = call(split_kernel, [chunk] * 4, scalars=3)(*place, keep, recv)
    parts = [parts[0]] + [xor_permute(parts[d], 16 * d) for d in range(1, 4)]
    part = (parts[0] + parts[1]) + (parts[2] + parts[3])
    for masks in ((2, 4, 6), (1, 64, 65)):
        near, mid, far = [xor_permute(part, m) for m in masks]
        part = (part + near) + (mid + far)
    pieces = [part] + [xor_permute(part, 16 * d) for d in range(1, 4)]
    (own,) = call(join_kernel, [half], scalars=3)(*place, *pieces)
    other = xor_permute(own, 8)
    grad_shape = jax.ShapeDtypeStruct((3, 3, 3, chans, chans), F32)

    (mine,) = call(functools.partial(unpack_own_kernel, scale=scale), [grad_shape], scalars=3)(*place, own)
    grad_one, grad_two = call(
        functools.partial(unpack_other_kernel, scale=scale),
        [grad_shape, grad_shape],
        [pltpu.VMEM(grad_shape.shape, F32), pltpu.SemaphoreType.DMA((2,))],
        scalars=3,
        inside=False,
    )(*place, mine, other)

    cuts = (0, tile_y // 4, tile_y // 2, tile_y)

    def rows_b(k):
        return [jax.ShapeDtypeStruct((tile_x, cuts[k + 1] - cuts[k], chans, tile_z), BF16)]

    piece, pre_pad = call(
        branch_first_kernel, rows_b(0) + [pad_b], scalars=3, flops=flops // 4
    )(*place, mask_f, w_branch, masked_grad, pre_grad, *pre_xr, *pre_yr)
    pieces = [piece]
    for k in (1, 2):
        kernel = functools.partial(branch_next_kernel, first=cuts[k])
        pieces += call(kernel, rows_b(k), flops=flops // 4 * k)(mask_f, w_branch, masked_grad, pre_pad)
    grad_features = jnp.transpose(jnp.concatenate(pieces, axis=1), (2, 0, 1, 3))
    return grad_features, grad_one, grad_two


def solution(mesh):
    placed = (P(None, "gx", "gy", None), P(None, "gx", "gy", None), P("gx", "gy", None), P(), P())
    return jax.shard_map(
        body,
        mesh=mesh,
        in_specs=placed,
        out_specs=(P(None, "gx", "gy", None), P(), P()),
        check_vma=False,
    )
```

```python
import functools
import math

import jax
import jax.numpy as jnp
from jax import lax
from jax.experimental import pallas as pl
from jax.experimental.pallas import tpu as pltpu
from jax.sharding import PartitionSpec as P


F32 = jnp.float32
BF16 = jnp.bfloat16
AXES = ("gx", "gy")


def swap_perms(count):
    even = [(i, i ^ 1) for i in range(count)]
    odd = [(i, i + 1 if i % 2 else i - 1) for i in range(1, count - 1)]
    return even, odd


def xor_permute(value, mask):
    total = lax.axis_size("gx") * lax.axis_size("gy")
    return lax.ppermute(value, AXES, [(i, i ^ mask) for i in range(total)])


def swap(value_even, value_odd, axis):
    even, odd = swap_perms(lax.axis_size(axis))
    return lax.ppermute(value_even, axis, even), lax.ppermute(value_odd, axis, odd)


def stack_row(stack, at_x, first_y, row):
    count, chans, depth = row.shape
    lane = lax.broadcasted_iota(jnp.int32, row.shape, 2)
    zero = jnp.zeros_like(row)
    below = jnp.where(lane == 0, zero, pltpu.roll(row, 1, 2))
    above = jnp.where(lane == depth - 1, zero, pltpu.roll(row, depth - 1, 2))
    ys = pl.ds(first_y, count)
    stack[at_x, ys, 0:chans, :] = below
    stack[at_x, ys, chans : 2 * chans, :] = row
    stack[at_x, ys, 2 * chans : 3 * chans, :] = above


def store_shifted(stack, x, y, value):
    chans, depth = value.shape
    lane = lax.broadcasted_iota(jnp.int32, value.shape, 1)
    below = jnp.where(lane == 0, 0.0, pltpu.roll(value, 1, 1))
    above = jnp.where(lane == depth - 1, 0.0, pltpu.roll(value, depth - 1, 1))
    stack[x, y, 0:chans] = below.astype(BF16)
    stack[x, y, chans : 2 * chans] = value.astype(BF16)
    stack[x, y, 2 * chans : 3 * chans] = above.astype(BF16)


def sides(parity, size):
    even = (1 - parity) * (size + 1)
    return even, size + 1 - even


def pad_tile(padded, place, tile, xr_even, xr_odd, yr_even, yr_odd, which):
    size_x, size_y = tile.shape[0], tile.shape[1]
    x_even, x_odd = sides(place[0], size_x)
    y_even, y_odd = sides(place[1], size_y)
    padded[x_even, 1 : size_y + 1] = xr_even[which]
    padded[x_odd, 1 : size_y + 1] = xr_odd[which]
    for i in range(size_x + 2):
        padded[i, y_even] = yr_even[i]
        padded[i, y_odd] = yr_odd[i]

    def body(i, carry):
        padded[i + 1, 1 : size_y + 1] = tile[i]
        return carry

    lax.fori_loop(0, size_x, body, 0)


def ypack_kernel(place, *refs):
    count = (len(refs) - 2) // 3
    tiles, (xr_even, xr_odd), outs = refs[:count], refs[count : count + 2], refs[count + 2 :]
    size_x, size_y = tiles[0].shape[0], tiles[0].shape[1]
    x_even, x_odd = sides(place[0], size_x)
    edges = (1 - place[1]) * (size_y - 1), place[1] * (size_y - 1)
    for k, tile in enumerate(tiles):
        for out, edge in zip(outs[2 * k : 2 * k + 2], edges):
            out[x_even] = xr_even[k, edge]
            out[x_odd] = xr_odd[k, edge]
            for i in range(size_x):
                out[i + 1] = tile[i, edge]


def conv_padded(padded, weights, first, count, emit):
    wide, _, chans, depth = padded.shape

    def body(x, carry):
        lane = lax.broadcasted_iota(jnp.int32, (chans, depth), 1)
        for y in range(first, first + count, 2):
            halves = []
            for side in range(2):
                at = y + side
                rows = [padded[x + a, at : at + 3].reshape(3 * chans, depth) for a in range(3)]
                halves.append(jnp.concatenate(rows, axis=0))
            out = jnp.dot(weights[...], jnp.concatenate(halves, axis=1), preferred_element_type=F32)
            for side in range(2):
                part = out[:, side * depth : (side + 1) * depth]
                below = jnp.where(lane == 0, 0.0, pltpu.roll(part[0:chans], 1, 1))
                above = jnp.where(lane == depth - 1, 0.0, pltpu.roll(part[2 * chans :], depth - 1, 1))
                emit(x, y + side, below + part[chans : 2 * chans] + above)
        return carry

    lax.fori_loop(0, wide - 2, body, 0, unroll=4)


def weights_kernel(one, two, w_pre, w_act, w_branch):
    chans = one.shape[-1]
    for kz in range(3):
        rows = slice(kz * chans, (kz + 1) * chans)
        taps = jnp.concatenate([one[a, b, kz] for a in range(3) for b in range(3)], axis=0)
        w_pre[rows] = taps.T
        for source, dest in ((two, w_act), (one, w_branch)):
            dest[rows] = jnp.concatenate(
                [source[2 - a, 2 - b, 2 - kz] for a in range(3) for b in range(3)], axis=1
            )


def forward_kernel(place, mask, weights, tile, xr_even, xr_odd, yr_even, yr_odd, activ, slope, padded):
    pad_tile(padded, place, tile, xr_even, xr_odd, yr_even, yr_odd, 0)

    def emit(x, y, value):
        sig = jax.nn.sigmoid(value)
        store_shifted(activ, x, y, mask[...] * (value * sig))
        slope[x, y] = mask[...] * (sig * (1.0 + value * (1.0 - sig)))

    conv_padded(padded, weights, 0, tile.shape[1], emit)


def backward_kernel(
    place, weights, slope, tile, xr_even, xr_odd, yr_even, yr_odd, pre_grad, xs_even, xs_odd, padded
):
    pad_tile(padded, place, tile, xr_even, xr_odd, yr_even, yr_odd, 1)
    size_x = tile.shape[0]

    def emit(x, y, value):
        pre_grad[x, y] = (slope[x, y] * value).astype(BF16)

    conv_padded(padded, weights, 0, tile.shape[1], emit)
    xs_even[0] = pre_grad[(1 - place[0]) * (size_x - 1)]
    xs_odd[0] = pre_grad[place[0] * (size_x - 1)]


def branch_part(mask, weights, base, padded, result, first):
    def emit(x, y, value):
        result[x, y - first] = (base[x, y].astype(F32) + mask[...] * value).astype(BF16)

    conv_padded(padded, weights, first, result.shape[1], emit)


def branch_first_kernel(place, mask, weights, base, tile, xr_even, xr_odd, yr_even, yr_odd, result, padded):
    pad_tile(padded, place, tile, xr_even, xr_odd, yr_even, yr_odd, 0)
    branch_part(mask, weights, base, padded, result, 0)


def branch_next_kernel(mask, weights, base, padded, result, *, first):
    branch_part(mask, weights, base, padded, result, first)


def grad_accumulate(padded, stack, acc):
    size_x, size_y, _, _ = stack.shape
    acc[...] = jnp.zeros_like(acc)

    def body(i, carry):
        right = jnp.concatenate([stack[i, y] for y in range(size_y)], axis=1)
        left = []
        for a in range(3):
            rows = [padded[i + a, y] for y in range(size_y + 2)]
            for b in range(3):
                left.append(jnp.concatenate(rows[b : b + size_y], axis=1))
        left = jnp.concatenate(left, axis=0)
        acc[...] += lax.dot_general(left, right, (((1,), (1,)), ((), ())), preferred_element_type=F32)
        return carry

    lax.fori_loop(0, size_x, body, 0, unroll=4)


def pack_grad(dest, acc, chans):
    rows = acc.shape[0]
    half = rows // 2
    dest[0:rows] = acc[:, 0 : 2 * chans]
    low = acc[0:half, 2 * chans : 3 * chans]
    high = acc[half:rows, 2 * chans : 3 * chans]
    dest[rows : rows + half] = jnp.concatenate([low, high], axis=1)


def stack_tile(stack, source):
    def body(i, carry):
        stack_row(stack, i, 0, source[i])
        return carry

    lax.fori_loop(0, source.shape[0], body, 0, unroll=4)


def grad_two_kernel(grad_pad, activ, packed, acc):
    grad_accumulate(grad_pad, activ, acc)
    pack_grad(packed, acc, grad_pad.shape[2])


def grad_one_kernel(place, in_pad, pre_grad, packed_two, keep, send, stack, acc):
    stack_tile(stack, pre_grad)
    grad_accumulate(in_pad, stack, acc)

    @pl.when(place[0] == 0)
    def _():
        pack_grad(keep, acc, pre_grad.shape[2])
        send[...] = packed_two[...]

    @pl.when(place[0] != 0)
    def _():
        pack_grad(send, acc, pre_grad.shape[2])
        keep[...] = packed_two[...]


def split_kernel(place, keep, recv, *outs):
    rows = outs[0].shape[0]
    for dist, out in enumerate(outs):
        start = pl.multiple_of((place[2] ^ dist) * rows, 8)
        out[...] = keep[pl.ds(start, rows)] + recv[pl.ds(start, rows)]


def join_kernel(place, *refs):
    out = refs[-1]
    rows = refs[0].shape[0]
    for dist, part in enumerate(refs[:-1]):
        start = pl.multiple_of((place[2] ^ dist) * rows, 8)
        out[pl.ds(start, rows)] = part[...]


def unpack(scale, source, dest, second):
    chans = dest.shape[-1]
    rows = 9 * chans
    half, step = rows // 2, chans // 2
    for a in range(3):
        for b in range(3):
            start = (3 * a + b) * chans
            both = source[start : start + chans, :] * scale
            pieces = []
            for first in (start, start + step):
                if first < half:
                    pieces.append(source[rows + first : rows + first + step, 0:chans])
                else:
                    pieces.append(source[rows + first - half : rows + first - half + step, chans : 2 * chans])
            tail = jnp.concatenate(pieces, axis=0) * scale
            if second:
                both = both.T
                dest[2 - a, 2 - b, 0] = both[0:chans]
                dest[2 - a, 2 - b, 1] = both[chans : 2 * chans]
                dest[2 - a, 2 - b, 2] = tail.T
            else:
                dest[a, b, 2] = both[:, 0:chans]
                dest[a, b, 1] = both[:, chans : 2 * chans]
                dest[a, b, 0] = tail


def unpack_own_kernel(place, own, dest, *, scale):
    @pl.when(place[0] == 0)
    def _():
        unpack(scale, own, dest, False)

    @pl.when(place[0] != 0)
    def _():
        unpack(scale, own, dest, True)


def unpack_other_kernel(place, mine, other, grad_one, grad_two, held, sems, *, scale):
    def finish(own_dest, other_dest, second):
        first = pltpu.make_async_copy(mine, own_dest, sems.at[0])
        first.start()
        unpack(scale, other, held, second)
        last = pltpu.make_async_copy(held, other_dest, sems.at[1])
        last.start()
        first.wait()
        last.wait()

    @pl.when(place[0] == 0)
    def _():
        finish(grad_one, grad_two, True)

    @pl.when(place[0] != 0)
    def _():
        finish(grad_two, grad_one, False)


def call(kernel, outs, scratch=(), scalars=0, flops=0, inside=True, after=0):
    def wrapped(*refs):
        refs = refs[: len(refs) - len(outs) - len(scratch) - after] + refs[len(refs) - len(outs) - len(scratch) :]
        if scalars:
            kernel([ref[0] for ref in refs[:scalars]], *refs[scalars:])
        else:
            kernel(*refs)

    def run(*operands):
        specs = [pl.BlockSpec(memory_space=pltpu.SMEM)] * scalars
        specs += [pl.BlockSpec(memory_space=pltpu.VMEM)] * (len(operands) - scalars - after)
        specs += [pl.BlockSpec(memory_space=pl.ANY)] * after
        moved = sum(o.size * o.dtype.itemsize for o in operands)
        moved += sum(math.prod(o.shape) * o.dtype.itemsize for o in outs)
        return pl.pallas_call(
            wrapped,
            out_shape=tuple(outs),
            in_specs=specs,
            out_specs=tuple(pl.BlockSpec(memory_space=pltpu.VMEM if inside else pl.ANY) for _ in outs),
            scratch_shapes=list(scratch),
            cost_estimate=pl.CostEstimate(flops=flops, bytes_accessed=moved, transcendentals=0),
            compiler_params=pltpu.CompilerParams(vmem_limit_bytes=40 * 1024 * 1024),
        )(*operands)

    return run


def body(features, cotangent, block_mask, kernel_one, kernel_two):
    chans, tile_x, tile_y, tile_z = features.shape
    blocks = block_mask.shape[2]
    cells_all = tile_x * tile_y * tile_z * lax.axis_size("gx") * lax.axis_size("gy")
    scale = 1.0 / math.sqrt(cells_all)
    place_x, place_y = lax.axis_index("gx"), lax.axis_index("gy")
    x_odd, y_odd = place_x & 1, place_y & 1
    place = [v.astype(jnp.int32).reshape(1) for v in (x_odd, y_odd, (place_x >> 1) & 3)]

    mask = jnp.broadcast_to(block_mask.reshape(blocks, 1), (blocks, tile_z // blocks)).reshape(1, tile_z)
    mask_f = mask.astype(F32)
    mask_b = mask.astype(BF16).reshape(1, 1, tile_z)

    def x_edges(at):
        both = [lax.dynamic_index_in_dim(a, at, 1, keepdims=False) * mask_b for a in (features, cotangent)]
        return jnp.stack([jnp.transpose(a, (1, 0, 2)) for a in both])

    xr = swap(x_edges((1 - x_odd) * (tile_x - 1)), x_edges(x_odd * (tile_x - 1)), "gx")
    masked_in = jnp.transpose(features * mask_b[:, None], (1, 2, 0, 3))
    masked_grad = jnp.transpose(cotangent * mask_b[:, None], (1, 2, 0, 3))

    tile_shape = (tile_x, tile_y, chans, tile_z)
    tile_b = jax.ShapeDtypeStruct(tile_shape, BF16)
    column_b = jax.ShapeDtypeStruct((tile_x + 2, chans, tile_z), BF16)
    edge_b = jax.ShapeDtypeStruct((1, tile_y, chans, tile_z), BF16)
    pad_b = jax.ShapeDtypeStruct((tile_x + 2, tile_y + 2, chans, tile_z), BF16)
    flops = 2 * 27 * chans * chans * tile_x * tile_y * tile_z

    def y_sends(tiles, halo_x):
        outs = [column_b] * (2 * len(tiles))
        return call(ypack_kernel, outs, scalars=3)(*place, *tiles, *halo_x)

    sends = y_sends((masked_in, masked_grad), xr)
    matrix = jax.ShapeDtypeStruct((3 * chans, 9 * chans), BF16)
    even, odd = swap_perms(lax.axis_size("gy"))
    in_even = lax.ppermute(sends[0], "gy", even)
    w_pre, w_act, w_branch = call(weights_kernel, [matrix] * 3)(kernel_one, kernel_two)
    in_next, w_pre = lax.optimization_barrier((sends[1], w_pre))
    in_odd = lax.ppermute(in_next, "gy", odd)
    in_y = (in_even, in_odd)
    grad_y = swap(*sends[2:], "gy")

    tile_s = pltpu.VMEM((tile_x, tile_y, 3 * chans, tile_z), BF16)
    shifted_b = jax.ShapeDtypeStruct((tile_x, tile_y, 3 * chans, tile_z), BF16)
    grad_s = pltpu.VMEM((9 * chans, 3 * chans), F32)

    activ, slope, in_pad = call(
        forward_kernel, [shifted_b, jax.ShapeDtypeStruct(tile_shape, F32), pad_b], scalars=3, flops=flops
    )(*place, mask_f, w_pre, masked_in, *xr, *in_y)
    pre_grad, xs_even, xs_odd, grad_pad = call(
        backward_kernel, [tile_b, edge_b, edge_b, pad_b], scalars=3, flops=flops
    )(*place, w_act, slope, masked_grad, *xr, *grad_y)

    packed = 27 * chans * chans // (2 * chans)
    half = jax.ShapeDtypeStruct((packed, 2 * chans), F32)
    pre_xr = swap(xs_even, xs_odd, "gx")
    (packed_two,) = call(grad_two_kernel, [half], [grad_s], flops=flops)(grad_pad, activ)
    pre_sends = y_sends((pre_grad,), pre_xr)
    pre_even = lax.ppermute(pre_sends[0], "gy", even)
    pre_odd = lax.ppermute(pre_sends[1], "gy", odd)
    pre_yr = (pre_even, pre_odd)
    keep, send = call(grad_one_kernel, [half, half], [tile_s, grad_s], scalars=3, flops=flops)(
        *place, in_pad, pre_grad, packed_two
    )

    recv = xor_permute(send, 8)
    chunk = jax.ShapeDtypeStruct((packed // 4, 2 * chans), F32)
    parts = call(split_kernel, [chunk] * 4, scalars=3)(*place, keep, recv)
    parts = [parts[0]] + [xor_permute(parts[d], 16 * d) for d in range(1, 4)]
    part = (parts[0] + parts[1]) + (parts[2] + parts[3])
    for masks in ((2, 4, 6), (1, 64, 65)):
        near, mid, far = [xor_permute(part, m) for m in masks]
        part = (part + near) + (mid + far)
    pieces = [part] + [xor_permute(part, 16 * d) for d in range(1, 4)]
    cuts = (0, tile_y // 4, 3 * tile_y // 4, tile_y)

    def rows_b(k):
        return [jax.ShapeDtypeStruct((tile_x, cuts[k + 1] - cuts[k], chans, tile_z), BF16)]

    piece, pre_pad = call(
        branch_first_kernel, rows_b(0) + [pad_b], scalars=3, flops=flops // 4
    )(*place, mask_f, w_branch, masked_grad, pre_grad, *pre_xr, *pre_yr)
    parts_y = [piece]
    for k in (1, 2):
        kernel = functools.partial(branch_next_kernel, first=cuts[k])
        parts_y += call(kernel, rows_b(k), flops=flops // 4)(mask_f, w_branch, masked_grad, pre_pad)
    grad_features = jnp.transpose(jnp.concatenate(parts_y, axis=1), (2, 0, 1, 3))
    (own,) = call(join_kernel, [half], scalars=3, after=1)(
        *place, *pieces, grad_features
    )
    other = xor_permute(own, 8)
    grad_shape = jax.ShapeDtypeStruct((3, 3, 3, chans, chans), F32)

    (mine,) = call(functools.partial(unpack_own_kernel, scale=scale), [grad_shape], scalars=3)(*place, own)
    grad_one, grad_two = call(
        functools.partial(unpack_other_kernel, scale=scale),
        [grad_shape, grad_shape],
        [pltpu.VMEM(grad_shape.shape, F32), pltpu.SemaphoreType.DMA((2,))],
        scalars=3,
        inside=False,
    )(*place, mine, other)

    return grad_features, grad_one, grad_two


def solution(mesh):
    placed = (P(None, "gx", "gy", None), P(None, "gx", "gy", None), P("gx", "gy", None), P(), P())
    return jax.shard_map(
        body,
        mesh=mesh,
        in_specs=placed,
        out_specs=(P(None, "gx", "gy", None), P(), P()),
        check_vma=False,
    )
```

```python
import functools
import math

import jax
import jax.numpy as jnp
from jax import lax
from jax.experimental import pallas as pl
from jax.experimental.pallas import tpu as pltpu
from jax.sharding import PartitionSpec as P


F32 = jnp.float32
BF16 = jnp.bfloat16
AXES = ("gx", "gy")


def swap_perms(count):
    even = [(i, i ^ 1) for i in range(count)]
    odd = [(i, i + 1 if i % 2 else i - 1) for i in range(1, count - 1)]
    return even, odd


def xor_permute(value, mask):
    total = lax.axis_size("gx") * lax.axis_size("gy")
    return lax.ppermute(value, AXES, [(i, i ^ mask) for i in range(total)])


def swap(value_even, value_odd, axis):
    even, odd = swap_perms(lax.axis_size(axis))
    return lax.ppermute(value_even, axis, even), lax.ppermute(value_odd, axis, odd)


def stack_row(stack, at_x, first_y, row):
    count, chans, depth = row.shape
    lane = lax.broadcasted_iota(jnp.int32, row.shape, 2)
    zero = jnp.zeros_like(row)
    below = jnp.where(lane == 0, zero, pltpu.roll(row, 1, 2))
    above = jnp.where(lane == depth - 1, zero, pltpu.roll(row, depth - 1, 2))
    ys = pl.ds(first_y, count)
    stack[at_x, ys, 0:chans, :] = below
    stack[at_x, ys, chans : 2 * chans, :] = row
    stack[at_x, ys, 2 * chans : 3 * chans, :] = above


def store_shifted(stack, x, y, value):
    chans, depth = value.shape
    lane = lax.broadcasted_iota(jnp.int32, value.shape, 1)
    below = jnp.where(lane == 0, 0.0, pltpu.roll(value, 1, 1))
    above = jnp.where(lane == depth - 1, 0.0, pltpu.roll(value, depth - 1, 1))
    stack[x, y, 0:chans] = below.astype(BF16)
    stack[x, y, chans : 2 * chans] = value.astype(BF16)
    stack[x, y, 2 * chans : 3 * chans] = above.astype(BF16)


def sides(parity, size):
    even = (1 - parity) * (size + 1)
    return even, size + 1 - even


def pad_tile(padded, place, tile, xr_even, xr_odd, yr_even, yr_odd, which):
    size_x, size_y = tile.shape[0], tile.shape[1]
    x_even, x_odd = sides(place[0], size_x)
    y_even, y_odd = sides(place[1], size_y)
    padded[x_even, 1 : size_y + 1] = xr_even[which]
    padded[x_odd, 1 : size_y + 1] = xr_odd[which]
    for i in range(size_x + 2):
        padded[i, y_even] = yr_even[i]
        padded[i, y_odd] = yr_odd[i]

    def body(i, carry):
        padded[i + 1, 1 : size_y + 1] = tile[i]
        return carry

    lax.fori_loop(0, size_x, body, 0)


def ypack_kernel(place, *refs):
    count = (len(refs) - 2) // 3
    tiles, (xr_even, xr_odd), outs = refs[:count], refs[count : count + 2], refs[count + 2 :]
    size_x, size_y = tiles[0].shape[0], tiles[0].shape[1]
    x_even, x_odd = sides(place[0], size_x)
    edges = (1 - place[1]) * (size_y - 1), place[1] * (size_y - 1)
    for k, tile in enumerate(tiles):
        for out, edge in zip(outs[2 * k : 2 * k + 2], edges):
            out[x_even] = xr_even[k, edge]
            out[x_odd] = xr_odd[k, edge]
            for i in range(size_x):
                out[i + 1] = tile[i, edge]


def conv_padded(padded, weights, first, count, emit):
    wide, _, chans, depth = padded.shape

    def body(x, carry):
        lane = lax.broadcasted_iota(jnp.int32, (chans, depth), 1)
        for y in range(first, first + count, 2):
            halves = []
            for side in range(2):
                at = y + side
                rows = [padded[x + a, at : at + 3].reshape(3 * chans, depth) for a in range(3)]
                halves.append(jnp.concatenate(rows, axis=0))
            out = jnp.dot(weights[...], jnp.concatenate(halves, axis=1), preferred_element_type=F32)
            for side in range(2):
                part = out[:, side * depth : (side + 1) * depth]
                below = jnp.where(lane == 0, 0.0, pltpu.roll(part[0:chans], 1, 1))
                above = jnp.where(lane == depth - 1, 0.0, pltpu.roll(part[2 * chans :], depth - 1, 1))
                emit(x, y + side, below + part[chans : 2 * chans] + above)
        return carry

    lax.fori_loop(0, wide - 2, body, 0, unroll=8)


def weights_kernel(one, two, w_pre, w_act, w_branch):
    chans = one.shape[-1]
    for kz in range(3):
        rows = slice(kz * chans, (kz + 1) * chans)
        taps = jnp.concatenate([one[a, b, kz] for a in range(3) for b in range(3)], axis=0)
        w_pre[rows] = taps.T
        for source, dest in ((two, w_act), (one, w_branch)):
            dest[rows] = jnp.concatenate(
                [source[2 - a, 2 - b, 2 - kz] for a in range(3) for b in range(3)], axis=1
            )


def forward_kernel(place, mask, weights, tile, xr_even, xr_odd, yr_even, yr_odd, activ, slope, padded):
    pad_tile(padded, place, tile, xr_even, xr_odd, yr_even, yr_odd, 0)

    def emit(x, y, value):
        sig = jax.nn.sigmoid(value)
        store_shifted(activ, x, y, mask[...] * (value * sig))
        slope[x, y] = mask[...] * (sig * (1.0 + value * (1.0 - sig)))

    conv_padded(padded, weights, 0, tile.shape[1], emit)


def backward_kernel(
    place, weights, slope, tile, xr_even, xr_odd, yr_even, yr_odd, pre_grad, xs_even, xs_odd, padded
):
    pad_tile(padded, place, tile, xr_even, xr_odd, yr_even, yr_odd, 1)
    size_x = tile.shape[0]

    def emit(x, y, value):
        pre_grad[x, y] = (slope[x, y] * value).astype(BF16)

    conv_padded(padded, weights, 0, tile.shape[1], emit)
    xs_even[0] = pre_grad[(1 - place[0]) * (size_x - 1)]
    xs_odd[0] = pre_grad[place[0] * (size_x - 1)]


def branch_part(mask, weights, base, padded, result, first):
    def emit(x, y, value):
        result[x, y - first] = (base[x, y].astype(F32) + mask[...] * value).astype(BF16)

    conv_padded(padded, weights, first, result.shape[1], emit)


def branch_first_kernel(place, mask, weights, base, tile, xr_even, xr_odd, yr_even, yr_odd, result, padded):
    pad_tile(padded, place, tile, xr_even, xr_odd, yr_even, yr_odd, 0)
    branch_part(mask, weights, base, padded, result, 0)


def branch_next_kernel(mask, weights, base, padded, result, *, first):
    branch_part(mask, weights, base, padded, result, first)


def grad_accumulate(padded, stack, acc):
    size_x, size_y, _, _ = stack.shape
    acc[...] = jnp.zeros_like(acc)

    def body(i, carry):
        right = jnp.concatenate([stack[i, y] for y in range(size_y)], axis=1)
        left = []
        for a in range(3):
            rows = [padded[i + a, y] for y in range(size_y + 2)]
            for b in range(3):
                left.append(jnp.concatenate(rows[b : b + size_y], axis=1))
        left = jnp.concatenate(left, axis=0)
        acc[...] += lax.dot_general(left, right, (((1,), (1,)), ((), ())), preferred_element_type=F32)
        return carry

    lax.fori_loop(0, size_x, body, 0, unroll=8)


def pack_grad(dest, acc, chans):
    rows = acc.shape[0]
    half = rows // 2
    dest[0:rows] = acc[:, 0 : 2 * chans]
    low = acc[0:half, 2 * chans : 3 * chans]
    high = acc[half:rows, 2 * chans : 3 * chans]
    dest[rows : rows + half] = jnp.concatenate([low, high], axis=1)


def stack_tile(stack, source):
    def body(i, carry):
        stack_row(stack, i, 0, source[i])
        return carry

    lax.fori_loop(0, source.shape[0], body, 0, unroll=8)


def grad_two_kernel(grad_pad, activ, packed, acc):
    grad_accumulate(grad_pad, activ, acc)
    pack_grad(packed, acc, grad_pad.shape[2])


def grad_one_kernel(place, in_pad, pre_grad, packed_two, keep, send, stack, acc):
    stack_tile(stack, pre_grad)
    grad_accumulate(in_pad, stack, acc)

    @pl.when(place[0] == 0)
    def _():
        pack_grad(keep, acc, pre_grad.shape[2])
        send[...] = packed_two[...]

    @pl.when(place[0] != 0)
    def _():
        pack_grad(send, acc, pre_grad.shape[2])
        keep[...] = packed_two[...]


def split_kernel(place, keep, recv, *outs):
    rows = outs[0].shape[0]
    for dist, out in enumerate(outs):
        start = pl.multiple_of((place[2] ^ dist) * rows, 8)
        out[...] = keep[pl.ds(start, rows)] + recv[pl.ds(start, rows)]


def join_kernel(place, *refs):
    out = refs[-1]
    rows = refs[0].shape[0]
    for dist, part in enumerate(refs[:-1]):
        start = pl.multiple_of((place[2] ^ dist) * rows, 8)
        out[pl.ds(start, rows)] = part[...]


def unpack(scale, source, dest, second):
    chans = dest.shape[-1]
    rows = 9 * chans
    half, step = rows // 2, chans // 2
    for a in range(3):
        for b in range(3):
            start = (3 * a + b) * chans
            both = source[start : start + chans, :] * scale
            pieces = []
            for first in (start, start + step):
                if first < half:
                    pieces.append(source[rows + first : rows + first + step, 0:chans])
                else:
                    pieces.append(source[rows + first - half : rows + first - half + step, chans : 2 * chans])
            tail = jnp.concatenate(pieces, axis=0) * scale
            if second:
                both = both.T
                dest[2 - a, 2 - b, 0] = both[0:chans]
                dest[2 - a, 2 - b, 1] = both[chans : 2 * chans]
                dest[2 - a, 2 - b, 2] = tail.T
            else:
                dest[a, b, 2] = both[:, 0:chans]
                dest[a, b, 1] = both[:, chans : 2 * chans]
                dest[a, b, 0] = tail


def unpack_own_kernel(place, own, dest, *, scale):
    @pl.when(place[0] == 0)
    def _():
        unpack(scale, own, dest, False)

    @pl.when(place[0] != 0)
    def _():
        unpack(scale, own, dest, True)


def unpack_other_kernel(place, mine, other, grad_one, grad_two, held, sems, *, scale):
    def finish(own_dest, other_dest, second):
        first = pltpu.make_async_copy(mine, own_dest, sems.at[0])
        first.start()
        unpack(scale, other, held, second)
        last = pltpu.make_async_copy(held, other_dest, sems.at[1])
        last.start()
        first.wait()
        last.wait()

    @pl.when(place[0] == 0)
    def _():
        finish(grad_one, grad_two, True)

    @pl.when(place[0] != 0)
    def _():
        finish(grad_two, grad_one, False)


def call(kernel, outs, scratch=(), scalars=0, flops=0, inside=True, after=0):
    def wrapped(*refs):
        refs = refs[: len(refs) - len(outs) - len(scratch) - after] + refs[len(refs) - len(outs) - len(scratch) :]
        if scalars:
            kernel([ref[0] for ref in refs[:scalars]], *refs[scalars:])
        else:
            kernel(*refs)

    def run(*operands):
        specs = [pl.BlockSpec(memory_space=pltpu.SMEM)] * scalars
        specs += [pl.BlockSpec(memory_space=pltpu.VMEM)] * (len(operands) - scalars - after)
        specs += [pl.BlockSpec(memory_space=pl.ANY)] * after
        moved = sum(o.size * o.dtype.itemsize for o in operands)
        moved += sum(math.prod(o.shape) * o.dtype.itemsize for o in outs)
        return pl.pallas_call(
            wrapped,
            out_shape=tuple(outs),
            in_specs=specs,
            out_specs=tuple(pl.BlockSpec(memory_space=pltpu.VMEM if inside else pl.ANY) for _ in outs),
            scratch_shapes=list(scratch),
            cost_estimate=pl.CostEstimate(flops=flops, bytes_accessed=moved, transcendentals=0),
            compiler_params=pltpu.CompilerParams(vmem_limit_bytes=40 * 1024 * 1024),
        )(*operands)

    return run


def body(features, cotangent, block_mask, kernel_one, kernel_two):
    chans, tile_x, tile_y, tile_z = features.shape
    blocks = block_mask.shape[2]
    cells_all = tile_x * tile_y * tile_z * lax.axis_size("gx") * lax.axis_size("gy")
    scale = 1.0 / math.sqrt(cells_all)
    place_x, place_y = lax.axis_index("gx"), lax.axis_index("gy")
    x_odd, y_odd = place_x & 1, place_y & 1
    place = [v.astype(jnp.int32).reshape(1) for v in (x_odd, y_odd, (place_x >> 1) & 3)]

    mask = jnp.broadcast_to(block_mask.reshape(blocks, 1), (blocks, tile_z // blocks)).reshape(1, tile_z)
    mask_f = mask.astype(F32)
    mask_b = mask.astype(BF16).reshape(1, 1, tile_z)

    def x_edges(at):
        both = [lax.dynamic_index_in_dim(a, at, 1, keepdims=False) * mask_b for a in (features, cotangent)]
        return jnp.stack([jnp.transpose(a, (1, 0, 2)) for a in both])

    xr = swap(x_edges((1 - x_odd) * (tile_x - 1)), x_edges(x_odd * (tile_x - 1)), "gx")
    masked_in = jnp.transpose(features * mask_b[:, None], (1, 2, 0, 3))
    masked_grad = jnp.transpose(cotangent * mask_b[:, None], (1, 2, 0, 3))

    tile_shape = (tile_x, tile_y, chans, tile_z)
    tile_b = jax.ShapeDtypeStruct(tile_shape, BF16)
    column_b = jax.ShapeDtypeStruct((tile_x + 2, chans, tile_z), BF16)
    edge_b = jax.ShapeDtypeStruct((1, tile_y, chans, tile_z), BF16)
    pad_b = jax.ShapeDtypeStruct((tile_x + 2, tile_y + 2, chans, tile_z), BF16)
    flops = 2 * 27 * chans * chans * tile_x * tile_y * tile_z

    def y_sends(tiles, halo_x):
        outs = [column_b] * (2 * len(tiles))
        return call(ypack_kernel, outs, scalars=3)(*place, *tiles, *halo_x)

    sends = y_sends((masked_in, masked_grad), xr)
    matrix = jax.ShapeDtypeStruct((3 * chans, 9 * chans), BF16)
    even, odd = swap_perms(lax.axis_size("gy"))
    in_even = lax.ppermute(sends[0], "gy", even)
    w_pre, w_act, w_branch = call(weights_kernel, [matrix] * 3)(kernel_one, kernel_two)
    in_next, w_pre = lax.optimization_barrier((sends[1], w_pre))
    in_odd = lax.ppermute(in_next, "gy", odd)
    in_y = (in_even, in_odd)
    grad_y = swap(*sends[2:], "gy")

    tile_s = pltpu.VMEM((tile_x, tile_y, 3 * chans, tile_z), BF16)
    shifted_b = jax.ShapeDtypeStruct((tile_x, tile_y, 3 * chans, tile_z), BF16)
    grad_s = pltpu.VMEM((9 * chans, 3 * chans), F32)

    activ, slope, in_pad = call(
        forward_kernel, [shifted_b, jax.ShapeDtypeStruct(tile_shape, F32), pad_b], scalars=3, flops=flops
    )(*place, mask_f, w_pre, masked_in, *xr, *in_y)
    pre_grad, xs_even, xs_odd, grad_pad = call(
        backward_kernel, [tile_b, edge_b, edge_b, pad_b], scalars=3, flops=flops
    )(*place, w_act, slope, masked_grad, *xr, *grad_y)

    packed = 27 * chans * chans // (2 * chans)
    half = jax.ShapeDtypeStruct((packed, 2 * chans), F32)
    pre_xr = swap(xs_even, xs_odd, "gx")
    (packed_two,) = call(grad_two_kernel, [half], [grad_s], flops=flops)(grad_pad, activ)
    pre_sends = y_sends((pre_grad,), pre_xr)
    pre_even = lax.ppermute(pre_sends[0], "gy", even)
    pre_odd = lax.ppermute(pre_sends[1], "gy", odd)
    pre_yr = (pre_even, pre_odd)
    keep, send = call(grad_one_kernel, [half, half], [tile_s, grad_s], scalars=3, flops=flops)(
        *place, in_pad, pre_grad, packed_two
    )

    recv = xor_permute(send, 8)
    chunk = jax.ShapeDtypeStruct((packed // 4, 2 * chans), F32)
    parts = call(split_kernel, [chunk] * 4, scalars=3)(*place, keep, recv)
    parts = [parts[0]] + [xor_permute(parts[d], 16 * d) for d in range(1, 4)]
    part = (parts[0] + parts[1]) + (parts[2] + parts[3])
    for masks in ((2, 4, 6), (1, 64, 65)):
        near, mid, far = [xor_permute(part, m) for m in masks]
        part = (part + near) + (mid + far)
    pieces = [part] + [xor_permute(part, 16 * d) for d in range(1, 4)]
    cuts = (0, tile_y // 4, 3 * tile_y // 4, tile_y)

    def rows_b(k):
        return [jax.ShapeDtypeStruct((tile_x, cuts[k + 1] - cuts[k], chans, tile_z), BF16)]

    piece, pre_pad = call(
        branch_first_kernel, rows_b(0) + [pad_b], scalars=3, flops=flops // 4
    )(*place, mask_f, w_branch, masked_grad, pre_grad, *pre_xr, *pre_yr)
    parts_y = [piece]
    for k in (1, 2):
        kernel = functools.partial(branch_next_kernel, first=cuts[k])
        parts_y += call(kernel, rows_b(k), flops=flops // 4)(mask_f, w_branch, masked_grad, pre_pad)
    grad_features = jnp.transpose(jnp.concatenate(parts_y, axis=1), (2, 0, 1, 3))
    (own,) = call(join_kernel, [half], scalars=3, after=1)(
        *place, *pieces, grad_features
    )
    other = xor_permute(own, 8)
    grad_shape = jax.ShapeDtypeStruct((3, 3, 3, chans, chans), F32)

    (mine,) = call(functools.partial(unpack_own_kernel, scale=scale), [grad_shape], scalars=3)(*place, own)
    grad_one, grad_two = call(
        functools.partial(unpack_other_kernel, scale=scale),
        [grad_shape, grad_shape],
        [pltpu.VMEM(grad_shape.shape, F32), pltpu.SemaphoreType.DMA((2,))],
        scalars=3,
        inside=False,
    )(*place, mine, other)

    return grad_features, grad_one, grad_two


def solution(mesh):
    placed = (P(None, "gx", "gy", None), P(None, "gx", "gy", None), P("gx", "gy", None), P(), P())
    return jax.shard_map(
        body,
        mesh=mesh,
        in_specs=placed,
        out_specs=(P(None, "gx", "gy", None), P(), P()),
        check_vma=False,
    )
```
